32 devices in a mesh: section: 2 (over x), dp: 16 (over z, y, core).
Axes of the slice: x: 2, y: 2, z: 4, core: 2. Of those that a mesh axis runs over, the one named last changes fastest.
Arguments:
- images: bfloat16 [64, 196, 768], P('dp'), may hold values from -6 to 6
- cotangent: bfloat16 [64, 196, 768], P('dp'), may hold values from -6 to 6
- w_qkv: bfloat16 [2, 768, 2304], P('section', 'dp'), may hold values from -0.21875 to 0.21875
- w_up: bfloat16 [2, 768, 3072], P('section', 'dp'), may hold values from -0.21875 to 0.21875
- w_proj: bfloat16 [2, 768, 768], P('section', 'dp'), may hold values from -1.75 to 1.75
- w_down: bfloat16 [2, 3072, 768], P('section', 'dp'), may hold values from -0.109375 to 0.109375
- ln_gain: float32 [2, 768], P('section'), may hold values from 0.1 to 1.9
- q_gain: float32 [2, 768], P('section'), may hold values from 0.1 to 1.9
- k_gain: float32 [2, 768], P('section'), may hold values from 0.1 to 1.9
Outputs:
- outputs: bfloat16 [2, 64, 196, 768], P('section', 'dp')
- input_grads: bfloat16 [2, 64, 196, 768], P('section', 'dp')
- grad_qkv: float32 [2, 768, 2304], P('section', 'dp')
- grad_up: float32 [2, 768, 3072], P('section', 'dp')
- grad_proj: float32 [2, 768, 768], P('section', 'dp')
- grad_down: float32 [2, 3072, 768], P('section', 'dp')
- grad_ln: float32 [2, 768], P('section')
- grad_q: float32 [2, 768], P('section')
- grad_k: float32 [2, 768], P('section')
The draws below stay inside these ranges and needn't reach their ends.
All inputs are finite; a program needn't handle non-finite values.
Results may differ from the reference program's by a relative error of at most 0.017.
Values may be sent and summed in bfloat16 or wider, within the bound.
No kernel may reach another device: no remote copies, remote signals or barrier semaphores. Data moves between devices by JAX's collectives and lax.ppermute only.
A program may use at most 320 MiB of HBM per device.

```python
import jax
import jax.numpy as jnp
from jax import lax

D = 768
HEADS = 12
HEAD = 64
FF = 3072
L = 196
IMG = 2
BATCH = 64


def shard_levels(stream_key, shape, split, smallest, top_value):
    level = 1.0
    for axis_at, parts in split:
        steps = jax.random.uniform(jax.random.fold_in(jax.random.fold_in(stream_key, 6), axis_at), (parts,), jnp.float32, smallest / len(split), top_value / len(split))
        level = level * jnp.repeat(jnp.exp(steps), shape[axis_at] // parts).reshape((-1,) + (1,) * (len(shape) - 1 - axis_at))
    return level


def scatter_about(own_key, dims, width, limit, cuts=(), kind=jnp.bfloat16):
    entries = jax.random.normal(own_key, dims, jnp.float32) * width
    if len(cuts) > 0:
        entries = shard_levels(own_key, dims, cuts, -0.22, 0.18) * entries
    return jnp.clip(entries, min=-limit, max=limit).astype(kind)


def setup_inputs(seed: int = 0) -> dict:
    key_of = jax.random.split(jax.random.key(seed), 10)
    return {
        "images": scatter_about(key_of[0], (BATCH, L, D), 1.0, 6.0, ((0, 16),)),
        "cotangent": scatter_about(key_of[1], (BATCH, L, D), 1.0, 6.0, ((0, 16),)),
        "w_qkv": scatter_about(key_of[2], (2, D, 3 * D), D ** -0.5, 0.21875, ((0, 2), (1, 16))),
        "w_up": scatter_about(key_of[3], (2, D, FF), D ** -0.5, 0.21875, ((0, 2), (1, 16))),
        "w_proj": scatter_about(key_of[4], (2, D, D), HEADS ** -0.5, 1.75, ((0, 2), (1, 16))),
        "w_down": scatter_about(key_of[5], (2, FF, D), FF ** -0.5, 0.109375, ((0, 2), (1, 16))),
        "ln_gain": jnp.clip(1.0 + 0.18 * jax.random.normal(key_of[6], (2, D), jnp.float32), 0.1, 1.9),
        "q_gain": jnp.clip(1.0 + 0.18 * jax.random.normal(key_of[7], (2, D), jnp.float32), 0.1, 1.9),
        "k_gain": jnp.clip(1.0 + 0.18 * jax.random.normal(key_of[8], (2, D), jnp.float32), 0.1, 1.9),
    }


@jax.custom_vjp
def low(v):
    return lax.optimization_barrier(v.astype(jnp.bfloat16)).astype(jnp.float32)

@jax.custom_vjp
def low_back(v):
    return v

def low_keep(v):
    return (low(v), None)

def low_pass(kept, grad):
    return (grad,)

def back_keep(v):
    return (v, None)

def back_low(kept, grad):
    return (low(grad),)
low.defvjp(low_keep, low_pass)
low_back.defvjp(back_keep, back_low)
EPSILON = 1e-06
HIGH = lax.Precision.HIGHEST

def layer_norm(values, gain):
    centred = values - lax.optimization_barrier(jnp.mean(values, axis=-1, keepdims=True))
    spread = lax.optimization_barrier(jnp.mean(centred * centred, axis=-1, keepdims=True))
    return centred * lax.rsqrt(spread + EPSILON) * gain

def head_norm(values, gain):
    shaped = values.reshape(values.shape[:-1] + (HEADS, HEAD))
    centred = shaped - lax.optimization_barrier(jnp.mean(shaped, axis=-1, keepdims=True))
    spread = lax.optimization_barrier(jnp.mean(centred * centred, axis=-1, keepdims=True))
    return (centred * lax.rsqrt(spread + EPSILON)).reshape(values.shape) * gain

def block(inputs, w_qkv, w_up, w_proj, w_down, ln_gain, q_gain, k_gain):
    count = inputs.shape[0]
    flat = inputs.reshape(count * L, D)
    normed = low(layer_norm(flat, ln_gain))
    qkv = low_back(jnp.dot(normed, w_qkv, precision=HIGH))
    query = low(head_norm(qkv[:, :D], q_gain)).reshape(count, L, HEADS, HEAD)
    key = low(head_norm(qkv[:, D:2 * D], k_gain)).reshape(count, L, HEADS, HEAD)
    value = low(qkv[:, 2 * D:]).reshape(count, L, HEADS, HEAD)
    scores = low_back(jnp.einsum('bqhd,bkhd->bhqk', query, key, precision=HIGH) * HEAD ** (-0.5))
    probs = low(jax.nn.softmax(scores, axis=-1))
    mixed = jnp.einsum('bhqk,bkhd->bqhd', probs, value, precision=HIGH).reshape(count * L, D)
    mixed = low_back(low(mixed))
    up_proj = low_back(jnp.dot(normed, w_up, precision=HIGH))
    hidden = low(jax.nn.gelu(up_proj, approximate=True))
    branch = jnp.dot(mixed, w_proj, precision=HIGH) + jnp.dot(hidden, w_down, precision=HIGH)
    return inputs + branch.reshape(inputs.shape)

def reference(images, cotangent, w_qkv, w_up, w_proj, w_down, ln_gain, q_gain, k_gain):
    params = [tuple((arr[s].astype(jnp.float32) for arr in (w_qkv, w_up, w_proj, w_down, ln_gain, q_gain, k_gain))) for s in range(2)]
    groups = BATCH // IMG
    grouped_in = images.reshape(groups, IMG, L, D)
    grouped_ct = cotangent.reshape(groups, IMG, L, D)

    def one_group(carry, item):
        inputs, tangent = item
        middle, pull_first = jax.vjp(block, inputs.astype(jnp.float32), *params[0])
        middle_low = middle.astype(jnp.bfloat16)
        final, pull_second = jax.vjp(block, middle_low.astype(jnp.float32), *params[1])
        grads_second = pull_second(tangent.astype(jnp.float32))
        back_middle = grads_second[0].astype(jnp.bfloat16)
        grads_first = pull_first(back_middle.astype(jnp.float32))
        carry = tuple((total + jnp.stack([first, second]) for total, first, second in zip(carry, grads_first[1:], grads_second[1:])))
        return (carry, (middle_low, final.astype(jnp.bfloat16), grads_first[0].astype(jnp.bfloat16), back_middle))
    start = tuple((jnp.zeros((2,) + p.shape, jnp.float32) for p in params[0]))
    totals, (middle_all, final_all, first_grads, middle_grads) = lax.scan(one_group, start, (grouped_in, grouped_ct))
    outputs = jnp.stack([middle_all.reshape(BATCH, L, D), final_all.reshape(BATCH, L, D)])
    input_grads = jnp.stack([first_grads.reshape(BATCH, L, D), middle_grads.reshape(BATCH, L, D)])
    return (outputs, input_grads, totals[0], totals[1], totals[2], totals[3], totals[4], totals[5], totals[6])
```

```python
from functools import partial

import jax
import jax.numpy as jnp
from jax import lax
from jax.experimental import pallas as pl
from jax.experimental.pallas import tpu as pltpu
from jax.sharding import PartitionSpec as P

D = 768
HEADS = 12
HEAD = 64
HALF = D // 2
PAIRS = HALF // 128
EPSILON = 1e-06
TILE = 256
BF = jnp.bfloat16
F32 = jnp.float32
C0 = 0.7978845608028654
C1 = 0.044715


def dot(a, b):
    return lax.dot_general(a, b, (((1,), (0,)), ((), ())), preferred_element_type=F32)


def dot_nt(a, b):
    return lax.dot_general(a, b, (((1,), (1,)), ((), ())), preferred_element_type=F32)


def dot_tn(a, b):
    return lax.dot_general(a, b, (((0,), (0,)), ((), ())), preferred_element_type=F32)


def head_means(x):
    row = lax.broadcasted_iota(jnp.int32, (256, 256), 0) // HEAD
    col = lax.broadcasted_iota(jnp.int32, (256, 256), 1) // HEAD
    ones = jnp.where(row == col, 1.0 / HEAD, 0.0).astype(BF)
    high = x.astype(BF)
    rest = (x - high.astype(F32)).astype(BF)
    parts = []
    for at in range(0, x.shape[1], 256):
        parts.append(dot(high[:, at : at + 256], ones) + dot(rest[:, at : at + 256], ones))
    return jnp.concatenate(parts, axis=1)


def half_mask(rows, h):
    return lax.broadcasted_iota(jnp.int32, (rows, 128), 1) // HEAD == h


def params(steps):
    return pltpu.CompilerParams(
        dimension_semantics=("arbitrary",) * steps, vmem_limit_bytes=56 * 1024 * 1024
    )


def attention_forward_kernel(
    tokens, sec, x_ref, w_ref, ln_ref, gain_ref, normed_ref, qk_ref, v_ref, r_ref, pt_ref, mixed_ref, part_ref
):
    section = sec[0]
    x = x_ref[...].astype(F32)
    rows = x.shape[0]
    pad = rows // 2
    centred = x - jnp.mean(x, axis=-1, keepdims=True)
    spread = jnp.mean(centred * centred, axis=-1, keepdims=True)
    normed = (centred * lax.rsqrt(spread + EPSILON) * ln_ref[...]).astype(BF)
    normed_ref[...] = normed
    qkv = dot(normed, w_ref[:, D:])
    qk = qkv[:, :D]
    centred = qk - head_means(qk)
    rstd = lax.rsqrt(head_means(centred * centred) + EPSILON)
    qk_ref[...] = (centred * rstd * gain_ref[...]).astype(BF)
    r_ref[...] = rstd.astype(BF)
    v_ref[...] = qkv[:, D:].astype(BF)
    valid = lax.broadcasted_iota(jnp.int32, (pad, pad), 0) < tokens
    for image in range(2):
        at = slice(image * pad, (image + 1) * pad)
        for pair in range(PAIRS):
            query = qk_ref[at, pair * 128 : (pair + 1) * 128]
            key = qk_ref[at, HALF + pair * 128 : HALF + (pair + 1) * 128]
            value = v_ref[at, pair * 128 : (pair + 1) * 128]
            mixed = jnp.zeros((pad, 128), F32)
            for h in range(2):
                mask = half_mask(pad, h)
                scores = dot_nt(jnp.where(mask, key, 0), query) * HEAD ** (-0.5)
                scores = jnp.where(valid, scores, -1e30)
                top = jnp.max(scores, axis=0, keepdims=True)
                weights = jnp.exp(scores - top)
                probs = weights * (1.0 / jnp.sum(weights, axis=0, keepdims=True))
                probs = probs.astype(BF)
                pt_ref[image, 2 * pair + h] = probs
                mixed += dot_tn(probs, jnp.where(mask, value, 0))
            mixed_ref[at, pair * 128 : (pair + 1) * 128] = mixed.astype(BF)
    proj = w_ref[pl.ds(pl.multiple_of(section * HALF, HALF), HALF), :D]
    part_ref[...] = dot(mixed_ref[...], proj).astype(BF)


def attention_forward(tokens, section, x, weights, ln_gain, qk_gain):
    rows = x.shape[0]
    images = rows // pad_of(tokens)
    pad = pad_of(tokens)
    step = 2 * pad
    row = lambda width: pl.BlockSpec((step, width), lambda i, s: (i, 0))
    full = lambda shape: pl.BlockSpec(shape, lambda i, s: (0, 0), pipeline_mode=pl.Buffered(1))
    return pl.pallas_call(
        partial(attention_forward_kernel, tokens),
        grid_spec=pltpu.PrefetchScalarGridSpec(
            num_scalar_prefetch=1,
            grid=(images // 2,),
            in_specs=[row(D), full((D, D + 3 * HALF)), full((1, D)), full((1, D))],
            out_specs=[
                row(D),
                row(D),
                row(HALF),
                row(D),
                pl.BlockSpec((2, 2 * PAIRS, pad, pad), lambda i, s: (i, 0, 0, 0)),
                row(HALF),
                row(D),
            ],
        ),
        out_shape=[
            jax.ShapeDtypeStruct((rows, D), BF),
            jax.ShapeDtypeStruct((rows, D), BF),
            jax.ShapeDtypeStruct((rows, HALF), BF),
            jax.ShapeDtypeStruct((rows, D), BF),
            jax.ShapeDtypeStruct((images, 2 * PAIRS, pad, pad), BF),
            jax.ShapeDtypeStruct((rows, HALF), BF),
            jax.ShapeDtypeStruct((rows, D), BF),
        ],
        compiler_params=params(1),
        cost_estimate=pl.CostEstimate(
            flops=2 * rows * D * (3 * HALF + HALF) + 8 * images * 6 * pad * pad * 64,
            bytes_accessed=rows * D * 12 + D * 1920 * 2,
            transcendentals=images * 6 * pad * pad,
        ),
        name="attention_forward",
    )(section, x, weights, ln_gain, qk_gain)


def feed_forward_kernel(steps, normed_ref, up_ref, down_ref, part_ref, hidden_ref, slope_ref, out_ref, acc_ref):
    step = pl.program_id(0)
    up = dot(normed_ref[...], up_ref[...])
    square = up * up
    tanh = jnp.tanh(C0 * up * (1.0 + C1 * square))
    hidden = (0.5 * up * (1.0 + tanh)).astype(BF)
    slope = 0.5 * (1.0 + tanh) + (0.5 * C0) * up * (1.0 - tanh * tanh) * (1.0 + (3.0 * C1) * square)
    hidden_ref[...] = hidden
    slope_ref[...] = slope.astype(BF)
    term = dot(hidden, down_ref[...])

    @pl.when(step == 0)
    def _():
        acc_ref[...] = part_ref[...].astype(F32) + term

    @pl.when(step > 0)
    def _():
        acc_ref[...] += term

    @pl.when(step == steps - 1)
    def _():
        out_ref[...] = acc_ref[...].astype(BF)


def up_spec():
    return pl.BlockSpec((D, TILE), lambda j: (0, j))


def down_spec(units):
    across = D // TILE
    return pl.BlockSpec((TILE, D), lambda j: (j % across, units // D + j // across))


def feed_forward(normed, weights, part):
    rows = normed.shape[0]
    units = weights.shape[1] // 2
    steps = units // TILE
    whole = pl.BlockSpec((rows, D), lambda j: (0, 0))
    tile = pl.BlockSpec((rows, TILE), lambda j: (0, j))
    return pl.pallas_call(
        partial(feed_forward_kernel, steps),
        grid=(steps,),
        in_specs=[whole, up_spec(), down_spec(units), whole],
        out_specs=[tile, tile, whole],
        out_shape=[
            jax.ShapeDtypeStruct((rows, units), BF),
            jax.ShapeDtypeStruct((rows, units), BF),
            jax.ShapeDtypeStruct((rows, D), BF),
        ],
        scratch_shapes=[pltpu.VMEM((rows, D), F32)],
        compiler_params=params(1),
        cost_estimate=pl.CostEstimate(
            flops=4 * rows * D * units,
            bytes_accessed=rows * D * 6 + rows * units * 4 + D * units * 4,
            transcendentals=rows * units,
        ),
        name="feed_forward",
    )(normed, weights, weights, part)


def feed_backward_kernel(steps, g_ref, normed_ref, up_ref, down_ref, hidden_ref, slope_ref, grad_ref, out_ref, acc_ref):
    step = pl.program_id(0)
    grad = g_ref[...]
    across = D // TILE
    d_up = (slope_ref[...].astype(F32) * dot_nt(grad, down_ref[...])).astype(BF)
    row = pl.multiple_of((step % across) * TILE, TILE)
    column = pl.multiple_of(steps * TILE + (step // across) * D, TILE)
    grad_ref[pl.ds(row, TILE), pl.ds(column, D)] = dot_tn(hidden_ref[...], grad).astype(BF)
    grad_ref[:, pl.ds(pl.multiple_of(step * TILE, TILE), TILE)] = dot_tn(normed_ref[...], d_up).astype(BF)
    term = dot_nt(d_up, up_ref[...])

    @pl.when(step == 0)
    def _():
        acc_ref[...] = term

    @pl.when(step > 0)
    def _():
        acc_ref[...] += term

    @pl.when(step == steps - 1)
    def _():
        out_ref[...] = acc_ref[...].astype(BF)


def feed_backward(grad, normed, weights, hidden, slope):
    rows = normed.shape[0]
    units = weights.shape[1] // 2
    steps = units // TILE
    whole = pl.BlockSpec((rows, D), lambda j: (0, 0))
    tile = pl.BlockSpec((rows, TILE), lambda j: (0, j))
    return pl.pallas_call(
        partial(feed_backward_kernel, steps),
        grid=(steps,),
        in_specs=[whole, whole, up_spec(), down_spec(units), tile, tile],
        out_specs=[pl.BlockSpec((D, 2 * units), lambda j: (0, 0)), whole],
        out_shape=[
            jax.ShapeDtypeStruct((D, 2 * units), BF),
            jax.ShapeDtypeStruct((rows, D), BF),
        ],
        scratch_shapes=[pltpu.VMEM((rows, D), F32)],
        compiler_params=params(1),
        cost_estimate=pl.CostEstimate(
            flops=8 * rows * D * units,
            bytes_accessed=rows * D * 6 + rows * units * 4 + D * units * 8,
            transcendentals=0,
        ),
        name="feed_backward",
    )(grad, normed, weights, weights, hidden, slope)


def attention_backward_kernel(
    steps,
    sec,
    g_ref,
    w_ref,
    gain_ref,
    inverse_ref,
    normed_ref,
    qk_ref,
    v_ref,
    r_ref,
    pt_ref,
    mixed_ref,
    ff_ref,
    grad_ref,
    out_ref,
    sums_ref,
    qkv_acc,
    proj_acc,
    d_qk,
    d_qkv,
):
    step = pl.program_id(0)
    section = sec[0]
    rows = g_ref.shape[0]
    pad = rows // 2

    @pl.when(step == 0)
    def _():
        sums_ref[...] = jnp.zeros_like(sums_ref)

    grad = g_ref[...]
    here = pl.ds(pl.multiple_of(section * HALF, HALF), HALF)
    d_mixed = dot_nt(grad, w_ref[here, :D]).astype(BF)
    proj_term = dot_tn(mixed_ref[...], grad)
    for image in range(2):
        at = slice(image * pad, (image + 1) * pad)
        for pair in range(PAIRS):
            lanes = slice(pair * 128, (pair + 1) * 128)
            key_lanes = slice(HALF + pair * 128, HALF + (pair + 1) * 128)
            query = qk_ref[at, lanes]
            key = qk_ref[at, key_lanes]
            value = v_ref[at, lanes]
            d_mix = d_mixed[at, lanes]
            d_query = jnp.zeros((pad, 128), F32)
            d_key = jnp.zeros((pad, 128), F32)
            d_value = jnp.zeros((pad, 128), F32)
            for h in range(2):
                mask = half_mask(pad, h)
                d_mix_head = jnp.where(mask, d_mix, 0)
                probs_low = pt_ref[image, 2 * pair + h]
                probs = probs_low.astype(F32)
                d_probs = dot_nt(value, d_mix_head)
                weighted = jnp.sum(probs * d_probs, axis=0, keepdims=True)
                d_scores = (probs * (d_probs - weighted)).astype(BF)
                d_value += dot(probs_low, d_mix_head)
                d_key += dot(d_scores, jnp.where(mask, query, 0))
                d_query += dot_tn(d_scores, jnp.where(mask, key, 0))
            d_qk[at, lanes] = d_query * HEAD ** (-0.5)
            d_qk[at, key_lanes] = d_key * HEAD ** (-0.5)
            d_qkv[at, D + pair * 128 : D + (pair + 1) * 128] = d_value.astype(BF)
    d_normed_heads = d_qk[...]
    shaped = qk_ref[...].astype(F32) * inverse_ref[...]
    sums_ref[1:2, :] += jnp.sum(d_normed_heads * shaped, axis=0, keepdims=True)
    scaled = d_normed_heads * gain_ref[...]
    d_qkv[:, :D] = (
        r_ref[...].astype(F32) * (scaled - head_means(scaled) - shaped * head_means(scaled * shaped))
    ).astype(BF)
    normed = normed_ref[...]
    qkv_term = dot_tn(normed, d_qkv[...])
    d_normed = dot_nt(d_qkv[...], w_ref[:, D:]) + ff_ref[...].astype(F32)
    out_ref[...] = d_normed.astype(BF)
    sums_ref[0:1, :] += jnp.sum(d_normed * normed.astype(F32), axis=0, keepdims=True)

    @pl.when(step == 0)
    def _():
        qkv_acc[...] = qkv_term
        proj_acc[...] = proj_term

    @pl.when(step > 0)
    def _():
        qkv_acc[...] += qkv_term
        proj_acc[...] += proj_term

    @pl.when(step == steps - 1)
    def _():
        there = pl.ds(pl.multiple_of((1 - section) * HALF, HALF), HALF)
        grad_ref[here, :D] = proj_acc[...].astype(BF)
        grad_ref[there, :D] = jnp.zeros((HALF, D), BF)
        grad_ref[:, D:] = qkv_acc[...].astype(BF)


def attention_backward(tokens, section, grad, weights, qk_gain, normed, qk, v, r, pt, mixed, ff):
    rows = normed.shape[0]
    pad = pad_of(tokens)
    images = rows // pad
    step = 2 * pad
    steps = images // 2
    width = weights.shape[1]
    row = lambda columns: pl.BlockSpec((step, columns), lambda i, s: (i, 0))
    full = lambda shape: pl.BlockSpec(shape, lambda i, s: (0, 0), pipeline_mode=pl.Buffered(1))
    return pl.pallas_call(
        partial(attention_backward_kernel, steps),
        grid_spec=pltpu.PrefetchScalarGridSpec(
            num_scalar_prefetch=1,
            grid=(steps,),
            in_specs=[
                row(D),
                full((D, width)),
                full((1, D)),
                full((1, D)),
                row(D),
                row(D),
                row(HALF),
                row(D),
                pl.BlockSpec((2, 2 * PAIRS, pad, pad), lambda i, s: (i, 0, 0, 0)),
                row(HALF),
                row(D),
            ],
            out_specs=[
                pl.BlockSpec((D, width), lambda i, s: (0, 0)),
                row(D),
                pl.BlockSpec((8, D), lambda i, s: (0, 0)),
            ],
            scratch_shapes=[
                pltpu.VMEM((D, 3 * HALF), F32),
                pltpu.VMEM((HALF, D), F32),
                pltpu.VMEM((step, D), F32),
                pltpu.VMEM((step, 3 * HALF), BF),
            ],
        ),
        out_shape=[
            jax.ShapeDtypeStruct((D, width), BF),
            jax.ShapeDtypeStruct((rows, D), BF),
            jax.ShapeDtypeStruct((8, D), F32),
        ],
        compiler_params=params(1),
        cost_estimate=pl.CostEstimate(
            flops=4 * rows * D * 4 * HALF + 16 * images * 6 * pad * pad * 64,
            bytes_accessed=rows * D * 16 + D * width * 4,
            transcendentals=0,
        ),
        name="attention_backward",
    )(section, grad, weights, qk_gain, 1.0 / qk_gain, normed, qk, v, r, pt, mixed, ff)


def norm_backward_kernel(g_ref, x_ref, mine_ref, theirs_ref, ln_ref, out_ref):
    x = x_ref[...].astype(F32)
    centred = x - jnp.mean(x, axis=-1, keepdims=True)
    rstd = lax.rsqrt(jnp.mean(centred * centred, axis=-1, keepdims=True) + EPSILON)
    shaped = centred * rstd
    scaled = (mine_ref[...].astype(F32) + theirs_ref[...].astype(F32)) * ln_ref[...]
    d_x = rstd * (
        scaled
        - jnp.mean(scaled, axis=-1, keepdims=True)
        - shaped * jnp.mean(scaled * shaped, axis=-1, keepdims=True)
    )
    out_ref[...] = (g_ref[...].astype(F32) + d_x).astype(BF)


def norm_backward(grad, x, mine, theirs, ln_gain):
    rows = x.shape[0]
    block = pl.BlockSpec((rows // 4, D), lambda i: (i, 0))
    return pl.pallas_call(
        norm_backward_kernel,
        grid=(4,),
        in_specs=[block] * 4 + [pl.BlockSpec((1, D), lambda i: (0, 0))],
        out_specs=block,
        out_shape=jax.ShapeDtypeStruct((rows, D), BF),
        compiler_params=params(1),
        cost_estimate=pl.CostEstimate(flops=12 * rows * D, bytes_accessed=rows * D * 10, transcendentals=0),
        name="norm_backward",
    )(grad, x, mine, theirs, ln_gain)


def pad_of(tokens):
    return -(-tokens // 16) * 16


def relative(value, step):
    count = lax.axis_size("dp")
    return lax.ppermute(value, "dp", [(source, source ^ step) for source in range(count)])


def gather_rows(shard):
    count = lax.axis_size("dp")
    me = lax.axis_index("dp")
    quads = [shard] + [relative(shard, 4 * far) for far in range(1, count // 4)]
    pieces = {4 * far: piece for far, piece in enumerate(quads)}
    pieces.update({4 * far + 2: relative(piece, 2) for far, piece in enumerate(quads)})
    pieces.update({step + 1: relative(piece, 1) for step, piece in list(pieces.items())})
    whole = jnp.zeros((count,) + shard.shape, shard.dtype)
    for step, piece in pieces.items():
        whole = lax.dynamic_update_slice(whole, piece[None], (me ^ step, 0, 0))
    return whole.reshape(count * shard.shape[0], shard.shape[1])


def add_low(left, right):
    return (left.astype(F32) + right.astype(F32)).astype(BF)


def scatter_rows(terms):
    count = lax.axis_size("dp")
    me = lax.axis_index("dp")
    core, near, far = me % 2, (me // 2) % 2, me // 4
    rows, width = terms.shape
    shaped = terms.reshape(count // 4, 2, 2, rows // count, width)
    pick = lambda value, at, axis: lax.dynamic_index_in_dim(value, at, axis, keepdims=False)
    total = add_low(pick(shaped, core, 2), relative(pick(shaped, 1 - core, 2), 1))
    total = add_low(pick(total, near, 1), relative(pick(total, 1 - near, 1), 2))
    result = pick(total, far, 0).astype(F32)
    for step in range(1, count // 4):
        result = result + relative(pick(total, far ^ step, 0), 4 * step).astype(F32)
    return result


def on_device(images, cotangent, w_qkv, w_up, w_proj, w_down, ln_gain, q_gain, k_gain):
    count = lax.axis_size("dp")
    section = lax.axis_index("section")
    first = section == 0
    scalar = section.astype(jnp.int32).reshape(1)
    number, tokens, _ = images.shape
    pad = pad_of(tokens)
    rows = w_qkv.shape[1]
    group = w_down.shape[1] // 4
    units = w_up.shape[2] // 2

    def swap(value):
        return lax.ppermute(value, "section", [(0, 1), (1, 0)])

    def give(value, source):
        return lax.ppermute(value, "section", [(source, 1 - source)])

    def half_of(half):
        parts = [w_proj[0]]
        for pair in range(3):
            at = pair * D + half * HALF
            parts.append(w_qkv[0, :, at : at + HALF])
        ups = w_up[0].reshape(rows, count, 4, group)
        for part in (2 * half, 2 * half + 1):
            parts.append(ups[:, :, part].reshape(rows, count * group))
        for part in (2 * half, 2 * half + 1):
            parts.append(w_down[0, part * group : (part + 1) * group])
        return jnp.concatenate(parts, axis=1)

    halves = (half_of(0), half_of(1))
    mine = jnp.where(first, halves[0], halves[1])
    other = swap(jnp.where(first, halves[1], halves[0]))
    shards = (jnp.where(first, mine, other), jnp.where(first, other, mine))
    split = D + 3 * HALF

    gains = []
    for gain in (ln_gain, q_gain, k_gain):
        theirs = swap(gain[0])
        gains.append((jnp.where(first, gain[0], theirs), jnp.where(first, theirs, gain[0])))
    at_half = lambda gain: lax.dynamic_slice_in_dim(gain, section * HALF, HALF, 0)
    ln_gains = [gain[None] for gain in gains[0]]
    qk_gains = [
        jnp.concatenate([at_half(gains[1][block]), at_half(gains[2][block])])[None] for block in range(2)
    ]

    def padded(value):
        return jnp.pad(value, ((0, 0), (0, pad - tokens), (0, 0))).reshape(number * pad, D)

    def trimmed(value):
        return value.reshape(number, pad, D)[:, :tokens]

    attention_weights, feed_weights, inputs, kept = [], [], [padded(images)], []
    parts = None
    for block in range(2):
        gathered = gather_rows(shards[block])
        attention_weights.append(gathered[:, :split])
        feed_weights.append(gathered[:, split:])
        saved = attention_forward(
            tokens, scalar, inputs[block], attention_weights[block], ln_gains[block], qk_gains[block]
        )
        hidden, slope, part = feed_forward(saved[0], feed_weights[block], saved[6])
        kept.append(tuple(saved[:6]) + (hidden, slope))
        theirs = swap(part) if block == 0 else give(part, 0)
        inputs.append(
            (inputs[block].astype(F32) + part.astype(F32) + theirs.astype(F32)).astype(BF)
        )
    outputs = trimmed(jnp.where(first, inputs[1], inputs[2]))

    grad = padded(cotangent)
    grads = [None, None]
    summed = [None, None]
    sums = [None, None]
    for block in (1, 0):
        normed, qk, v, r, pt, mixed, hidden, slope = kept[block]
        feed_grads, feed_part = feed_backward(grad, normed, feed_weights[block], hidden, slope)
        attention_grads, part, sums[block] = attention_backward(
            tokens, scalar, grad, attention_weights[block], qk_gains[block], normed, qk, v, r, pt, mixed, feed_part
        )
        theirs = swap(part) if block == 1 else give(part, 1)
        grad = norm_backward(grad, inputs[block], part, theirs, ln_gains[block])
        grads[block] = grad
        summed[block] = jnp.concatenate([scatter_rows(attention_grads), scatter_rows(feed_grads)], axis=1)
    input_grads = trimmed(jnp.where(first, grads[0], grads[1]))

    own = jnp.where(first, summed[0], summed[1])
    theirs = swap(jnp.where(first, summed[1], summed[0]).astype(BF)).astype(F32)
    low_half = jnp.where(first, own, theirs)
    high_half = jnp.where(first, theirs, own)
    grad_proj = own[:, :D] + theirs[:, :D]
    pieces = []
    for pair in range(3):
        at = slice(D + pair * HALF, D + (pair + 1) * HALF)
        pieces += [low_half[:, at], high_half[:, at]]
    grad_qkv = jnp.concatenate(pieces, axis=1)
    ups, downs = [], []
    for source in (low_half, high_half):
        for part in range(2):
            at = split + part * D
            ups.append(source[:, at : at + D].reshape(rows, count, 1, group))
            at = split + units + part * D
            downs.append(source[:, at : at + D])
    grad_up = jnp.concatenate(ups, axis=2).reshape(rows, 2 * units)
    grad_down = jnp.concatenate(downs, axis=0)

    gain_rows = []
    for block in range(2):
        zero = jnp.zeros((D,), F32)
        place = lambda value: lax.dynamic_update_slice_in_dim(zero, value, section * HALF, 0)
        gain_rows += [
            sums[block][0] / gains[0][block],
            place(sums[block][1, :HALF]),
            place(sums[block][1, HALF:]),
        ]
    totals = lax.psum(jnp.stack(gain_rows), ("section", "dp"))
    totals = jnp.where(first, totals[:3], totals[3:])
    return (
        outputs[None],
        input_grads[None],
        grad_qkv[None],
        grad_up[None],
        grad_proj[None],
        grad_down[None],
        totals[0:1],
        totals[1:2],
        totals[2:3],
    )


def solution(mesh):
    placed = (
        P("dp", None, None),
        P("dp", None, None),
        P("section", "dp", None),
        P("section", "dp", None),
        P("section", "dp", None),
        P("section", "dp", None),
        P("section", None),
        P("section", None),
        P("section", None),
    )
    return jax.shard_map(
        on_device,
        mesh=mesh,
        in_specs=placed,
        out_specs=(
            P("section", "dp", None, None),
            P("section", "dp", None, None),
            P("section", "dp", None),
            P("section", "dp", None),
            P("section", "dp", None),
            P("section", "dp", None),
            P("section", None),
            P("section", None),
            P("section", None),
        ),
        check_vma=False,
    )
```

```python
from functools import partial

import jax
import jax.numpy as jnp
from jax import lax
from jax.experimental import pallas as pl
from jax.experimental.pallas import tpu as pltpu
from jax.sharding import PartitionSpec as P

D = 768
HEADS = 12
HEAD = 64
HALF = D // 2
PAIRS = HALF // 128
EPSILON = 1e-06
TILE = 256
BF = jnp.bfloat16
F32 = jnp.float32
SPLIT = D + 3 * HALF
ANYWHERE = pl.BlockSpec(memory_space=pl.ANY)
C0 = 0.7978845608028654
C1 = 0.044715


def dot(a, b):
    return lax.dot_general(a, b, (((1,), (0,)), ((), ())), preferred_element_type=F32)


def dot_nt(a, b):
    return lax.dot_general(a, b, (((1,), (1,)), ((), ())), preferred_element_type=F32)


def dot_tn(a, b):
    return lax.dot_general(a, b, (((0,), (0,)), ((), ())), preferred_element_type=F32)


def head_means(x):
    row = lax.broadcasted_iota(jnp.int32, (256, 256), 0) // HEAD
    col = lax.broadcasted_iota(jnp.int32, (256, 256), 1) // HEAD
    ones = jnp.where(row == col, 1.0 / HEAD, 0.0).astype(BF)
    high = x.astype(BF)
    rest = (x - high.astype(F32)).astype(BF)
    parts = []
    for at in range(0, x.shape[1], 256):
        parts.append(dot(high[:, at : at + 256], ones) + dot(rest[:, at : at + 256], ones))
    return jnp.concatenate(parts, axis=1)


def half_mask(rows, h):
    return lax.broadcasted_iota(jnp.int32, (rows, 128), 1) // HEAD == h


def params(steps):
    return pltpu.CompilerParams(
        dimension_semantics=("arbitrary",) * steps, vmem_limit_bytes=20 * 1024 * 1024
    )


def copies(place, pieces, columns, dest_ref, sems):
    made = []
    for step, piece in enumerate(pieces):
        rows = piece.shape[0]
        at = pl.ds(pl.multiple_of((place[1] ^ step) * rows, rows), rows)
        made.append(pltpu.make_async_copy(piece.at[:, columns], dest_ref.at[at, :], sems.at[step]))
    return made


def attention_forward_kernel(tokens, count, place, *refs):
    pieces = refs[:count]
    (
        x_ref,
        ln_ref,
        gain_ref,
        normed_ref,
        qk_ref,
        v_ref,
        r_ref,
        pt_ref,
        mixed_ref,
        part_ref,
        w_ref,
        sems,
    ) = refs[count:]
    section = place[0]

    @pl.when(pl.program_id(0) == 0)
    def _():
        for copy in copies(place, pieces, slice(0, SPLIT), w_ref, sems):
            copy.start()

    x = x_ref[...].astype(F32)
    rows = x.shape[0]
    pad = rows // 2
    centred = x - jnp.mean(x, axis=-1, keepdims=True)
    spread = jnp.mean(centred * centred, axis=-1, keepdims=True)
    normed = (centred * lax.rsqrt(spread + EPSILON) * ln_ref[...]).astype(BF)
    normed_ref[...] = normed

    @pl.when(pl.program_id(0) == 0)
    def _():
        for copy in copies(place, pieces, slice(0, SPLIT), w_ref, sems):
            copy.wait()

    qkv = dot(normed, w_ref[:, D:])
    qk = qkv[:, :D]
    centred = qk - head_means(qk)
    rstd = lax.rsqrt(head_means(centred * centred) + EPSILON)
    qk_ref[...] = (centred * rstd * gain_ref[...]).astype(BF)
    r_ref[...] = rstd.astype(BF)
    v_ref[...] = qkv[:, D:].astype(BF)
    valid = lax.broadcasted_iota(jnp.int32, (pad, pad), 0) < tokens
    for image in range(2):
        at = slice(image * pad, (image + 1) * pad)
        for pair in range(PAIRS):
            query = qk_ref[at, pair * 128 : (pair + 1) * 128]
            key = qk_ref[at, HALF + pair * 128 : HALF + (pair + 1) * 128]
            value = v_ref[at, pair * 128 : (pair + 1) * 128]
            mixed = jnp.zeros((pad, 128), F32)
            for h in range(2):
                mask = half_mask(pad, h)
                scores = dot_nt(jnp.where(mask, key, 0), query) * HEAD ** (-0.5)
                scores = jnp.where(valid, scores, -1e30)
                top = jnp.max(scores, axis=0, keepdims=True)
                weights = jnp.exp(scores - top)
                probs = weights * (1.0 / jnp.sum(weights, axis=0, keepdims=True))
                probs = probs.astype(BF)
                pt_ref[image, 2 * pair + h] = probs
                mixed += dot_tn(probs, jnp.where(mask, value, 0))
            mixed_ref[at, pair * 128 : (pair + 1) * 128] = mixed.astype(BF)
    proj = w_ref[pl.ds(pl.multiple_of(section * HALF, HALF), HALF), :D]
    part_ref[...] = dot(mixed_ref[...], proj).astype(BF)


def attention_forward(tokens, place, x, pieces, ln_gain, qk_gain):
    rows = x.shape[0]
    images = rows // pad_of(tokens)
    pad = pad_of(tokens)
    step = 2 * pad
    row = lambda width: pl.BlockSpec((step, width), lambda i, s: (i, 0))
    full = lambda shape: pl.BlockSpec(shape, lambda i, s: (0, 0), pipeline_mode=pl.Buffered(1))
    return pl.pallas_call(
        partial(attention_forward_kernel, tokens, len(pieces)),
        grid_spec=pltpu.PrefetchScalarGridSpec(
            num_scalar_prefetch=1,
            grid=(images // 2,),
            in_specs=[ANYWHERE] * len(pieces) + [row(D), full((1, D)), full((1, D))],
            out_specs=[
                row(D),
                row(D),
                row(HALF),
                row(D),
                pl.BlockSpec((2, 2 * PAIRS, pad, pad), lambda i, s: (i, 0, 0, 0)),
                row(HALF),
                row(D),
            ],
            scratch_shapes=[
                pltpu.VMEM((D, SPLIT), BF),
                pltpu.SemaphoreType.DMA((len(pieces),)),
            ],
        ),
        out_shape=[
            jax.ShapeDtypeStruct((rows, D), BF),
            jax.ShapeDtypeStruct((rows, D), BF),
            jax.ShapeDtypeStruct((rows, HALF), BF),
            jax.ShapeDtypeStruct((rows, D), BF),
            jax.ShapeDtypeStruct((images, 2 * PAIRS, pad, pad), BF),
            jax.ShapeDtypeStruct((rows, HALF), BF),
            jax.ShapeDtypeStruct((rows, D), BF),
        ],
        compiler_params=params(1),
        cost_estimate=pl.CostEstimate(
            flops=2 * rows * D * (3 * HALF + HALF) + 8 * images * 6 * pad * pad * 64,
            bytes_accessed=rows * D * 12 + D * 1920 * 2,
            transcendentals=images * 6 * pad * pad,
        ),
        name="attention_forward",
    )(place, *pieces, x, ln_gain, qk_gain)


def feed_copies(place, pieces, units, up_ref, down_ref, sems):
    base = pieces[0].shape[1] - 2 * units
    ups = copies(place, pieces, slice(base, base + units), up_ref, sems.at[0])
    downs = []
    for part in range(units // D):
        columns = slice(base + units + part * D, base + units + (part + 1) * D)
        downs += copies(place, pieces, columns, down_ref.at[part], sems.at[1 + part])
    return ups, downs


def feed_tiles(step):
    across = D // TILE
    columns = pl.ds(pl.multiple_of(step * TILE, TILE), TILE)
    return columns, step // across, pl.ds(pl.multiple_of((step % across) * TILE, TILE), TILE)


def feed_forward_kernel(steps, count, place, *refs):
    pieces = refs[:count]
    normed_ref, part_ref, hidden_ref, slope_ref, out_ref, acc_ref, up_ref, down_ref, sems = refs[count:]
    step = pl.program_id(0)
    columns, part, rows = feed_tiles(step)

    @pl.when(step == 0)
    def _():
        ups, downs = feed_copies(place, pieces, steps * TILE, up_ref, down_ref, sems)
        for copy in ups + downs:
            copy.start()
        for copy in ups + downs:
            copy.wait()

    up = dot(normed_ref[...], up_ref[:, columns])
    square = up * up
    tanh = jnp.tanh(C0 * up * (1.0 + C1 * square))
    hidden = (0.5 * up * (1.0 + tanh)).astype(BF)
    slope = 0.5 * (1.0 + tanh) + (0.5 * C0) * up * (1.0 - tanh * tanh) * (1.0 + (3.0 * C1) * square)
    hidden_ref[...] = hidden
    slope_ref[...] = slope.astype(BF)
    term = dot(hidden, down_ref[part, rows, :])

    @pl.when(step == 0)
    def _():
        acc_ref[...] = part_ref[...].astype(F32) + term

    @pl.when(step > 0)
    def _():
        acc_ref[...] += term

    @pl.when(step == steps - 1)
    def _():
        out_ref[...] = acc_ref[...].astype(BF)


def feed_scratch(rows, units, count):
    return [
        pltpu.VMEM((rows, D), F32),
        pltpu.VMEM((D, units), BF),
        pltpu.VMEM((units // D, D, D), BF),
        pltpu.SemaphoreType.DMA((1 + units // D, count)),
    ]


def feed_forward(place, units, normed, pieces, part):
    rows = normed.shape[0]
    steps = units // TILE
    whole = pl.BlockSpec((rows, D), lambda j, s: (0, 0))
    tile = pl.BlockSpec((rows, TILE), lambda j, s: (0, j))
    return pl.pallas_call(
        partial(feed_forward_kernel, steps, len(pieces)),
        grid_spec=pltpu.PrefetchScalarGridSpec(
            num_scalar_prefetch=1,
            grid=(steps,),
            in_specs=[ANYWHERE] * len(pieces) + [whole, whole],
            out_specs=[tile, tile, whole],
            scratch_shapes=feed_scratch(rows, units, len(pieces)),
        ),
        out_shape=[
            jax.ShapeDtypeStruct((rows, units), BF),
            jax.ShapeDtypeStruct((rows, units), BF),
            jax.ShapeDtypeStruct((rows, D), BF),
        ],
        compiler_params=params(1),
        cost_estimate=pl.CostEstimate(
            flops=4 * rows * D * units,
            bytes_accessed=rows * D * 6 + rows * units * 4 + D * units * 4,
            transcendentals=rows * units,
        ),
        name="feed_forward",
    )(place, *pieces, normed, part)


def feed_backward_kernel(steps, count, place, *refs):
    pieces = refs[:count]
    g_ref, normed_ref, hidden_ref, slope_ref, grad_ref, out_ref, acc_ref, up_ref, down_ref, sems = refs[count:]
    step = pl.program_id(0)
    columns, part, rows = feed_tiles(step)

    @pl.when(step == 0)
    def _():
        ups, downs = feed_copies(place, pieces, steps * TILE, up_ref, down_ref, sems)
        for copy in downs + ups:
            copy.start()
        for copy in downs + ups:
            copy.wait()

    grad = g_ref[...]
    d_up = (slope_ref[...].astype(F32) * dot_nt(grad, down_ref[part, rows, :])).astype(BF)
    there = pl.ds(pl.multiple_of(steps * TILE + part * D, D), D)
    grad_ref[rows, there] = dot_tn(hidden_ref[...], grad).astype(BF)
    grad_ref[:, columns] = dot_tn(normed_ref[...], d_up).astype(BF)
    term = dot_nt(d_up, up_ref[:, columns])

    @pl.when(step == 0)
    def _():
        acc_ref[...] = term

    @pl.when(step > 0)
    def _():
        acc_ref[...] += term

    @pl.when(step == steps - 1)
    def _():
        out_ref[...] = acc_ref[...].astype(BF)


def feed_backward(place, units, grad, normed, pieces, hidden, slope):
    rows = normed.shape[0]
    steps = units // TILE
    whole = pl.BlockSpec((rows, D), lambda j, s: (0, 0))
    tile = pl.BlockSpec((rows, TILE), lambda j, s: (0, j))
    return pl.pallas_call(
        partial(feed_backward_kernel, steps, len(pieces)),
        grid_spec=pltpu.PrefetchScalarGridSpec(
            num_scalar_prefetch=1,
            grid=(steps,),
            in_specs=[ANYWHERE] * len(pieces) + [whole, whole, tile, tile],
            out_specs=[pl.BlockSpec((D, 2 * units), lambda j, s: (0, 0)), whole],
            scratch_shapes=feed_scratch(rows, units, len(pieces)),
        ),
        out_shape=[
            jax.ShapeDtypeStruct((D, 2 * units), BF),
            jax.ShapeDtypeStruct((rows, D), BF),
        ],
        compiler_params=params(1),
        cost_estimate=pl.CostEstimate(
            flops=8 * rows * D * units,
            bytes_accessed=rows * D * 6 + rows * units * 4 + D * units * 8,
            transcendentals=0,
        ),
        name="feed_backward",
    )(place, *pieces, grad, normed, hidden, slope)


def attention_backward_kernel(steps, count, place, *refs):
    pieces = refs[:count]
    (
        g_ref,
        gain_ref,
        inverse_ref,
        normed_ref,
        qk_ref,
        v_ref,
        r_ref,
        pt_ref,
        mixed_ref,
        ff_ref,
        grad_ref,
        out_ref,
        sums_ref,
        qkv_acc,
        proj_acc,
        d_qk,
        d_qkv,
        w_ref,
        sems,
    ) = refs[count:]
    step = pl.program_id(0)
    section = place[0]
    rows = g_ref.shape[0]
    pad = rows // 2

    @pl.when(step == 0)
    def _():
        for copy in copies(place, pieces, slice(0, SPLIT), w_ref, sems):
            copy.start()
        sums_ref[...] = jnp.zeros_like(sums_ref)
        for copy in copies(place, pieces, slice(0, SPLIT), w_ref, sems):
            copy.wait()

    grad = g_ref[...]
    here = pl.ds(pl.multiple_of(section * HALF, HALF), HALF)
    d_mixed = dot_nt(grad, w_ref[here, :D]).astype(BF)
    proj_term = dot_tn(mixed_ref[...], grad)
    for image in range(2):
        at = slice(image * pad, (image + 1) * pad)
        for pair in range(PAIRS):
            lanes = slice(pair * 128, (pair + 1) * 128)
            key_lanes = slice(HALF + pair * 128, HALF + (pair + 1) * 128)
            query = qk_ref[at, lanes]
            key = qk_ref[at, key_lanes]
            value = v_ref[at, lanes]
            d_mix = d_mixed[at, lanes]
            d_query = jnp.zeros((pad, 128), F32)
            d_key = jnp.zeros((pad, 128), F32)
            d_value = jnp.zeros((pad, 128), F32)
            for h in range(2):
                mask = half_mask(pad, h)
                d_mix_head = jnp.where(mask, d_mix, 0)
                probs_low = pt_ref[image, 2 * pair + h]
                probs = probs_low.astype(F32)
                d_probs = dot_nt(value, d_mix_head)
                weighted = jnp.sum(probs * d_probs, axis=0, keepdims=True)
                d_scores = (probs * (d_probs - weighted)).astype(BF)
                d_value += dot(probs_low, d_mix_head)
                d_key += dot(d_scores, jnp.where(mask, query, 0))
                d_query += dot_tn(d_scores, jnp.where(mask, key, 0))
            d_qk[at, lanes] = d_query * HEAD ** (-0.5)
            d_qk[at, key_lanes] = d_key * HEAD ** (-0.5)
            d_qkv[at, D + pair * 128 : D + (pair + 1) * 128] = d_value.astype(BF)
    d_normed_heads = d_qk[...]
    shaped = qk_ref[...].astype(F32) * inverse_ref[...]
    sums_ref[1:2, :] += jnp.sum(d_normed_heads * shaped, axis=0, keepdims=True)
    scaled = d_normed_heads * gain_ref[...]
    d_qkv[:, :D] = (
        r_ref[...].astype(F32) * (scaled - head_means(scaled) - shaped * head_means(scaled * shaped))
    ).astype(BF)
    normed = normed_ref[...]
    qkv_term = dot_tn(normed, d_qkv[...])
    d_normed = dot_nt(d_qkv[...], w_ref[:, D:]) + ff_ref[...].astype(F32)
    out_ref[...] = d_normed.astype(BF)
    sums_ref[0:1, :] += jnp.sum(d_normed * normed.astype(F32), axis=0, keepdims=True)

    @pl.when(step == 0)
    def _():
        qkv_acc[...] = qkv_term
        proj_acc[...] = proj_term

    @pl.when(step > 0)
    def _():
        qkv_acc[...] += qkv_term
        proj_acc[...] += proj_term

    @pl.when(step == steps - 1)
    def _():
        there = pl.ds(pl.multiple_of((1 - section) * HALF, HALF), HALF)
        grad_ref[here, :D] = proj_acc[...].astype(BF)
        grad_ref[there, :D] = jnp.zeros((HALF, D), BF)
        grad_ref[:, D:] = qkv_acc[...].astype(BF)


def attention_backward(tokens, place, grad, pieces, qk_gain, normed, qk, v, r, pt, mixed, ff):
    rows = normed.shape[0]
    pad = pad_of(tokens)
    images = rows // pad
    step = 2 * pad
    steps = images // 2
    width = SPLIT
    row = lambda columns: pl.BlockSpec((step, columns), lambda i, s: (i, 0))
    full = lambda shape: pl.BlockSpec(shape, lambda i, s: (0, 0), pipeline_mode=pl.Buffered(1))
    return pl.pallas_call(
        partial(attention_backward_kernel, steps, len(pieces)),
        grid_spec=pltpu.PrefetchScalarGridSpec(
            num_scalar_prefetch=1,
            grid=(steps,),
            in_specs=[ANYWHERE] * len(pieces)
            + [
                row(D),
                full((1, D)),
                full((1, D)),
                row(D),
                row(D),
                row(HALF),
                row(D),
                pl.BlockSpec((2, 2 * PAIRS, pad, pad), lambda i, s: (i, 0, 0, 0)),
                row(HALF),
                row(D),
            ],
            out_specs=[
                pl.BlockSpec((D, width), lambda i, s: (0, 0)),
                row(D),
                pl.BlockSpec((8, D), lambda i, s: (0, 0)),
            ],
            scratch_shapes=[
                pltpu.VMEM((D, 3 * HALF), F32),
                pltpu.VMEM((HALF, D), F32),
                pltpu.VMEM((step, D), F32),
                pltpu.VMEM((step, 3 * HALF), BF),
                pltpu.VMEM((D, SPLIT), BF),
                pltpu.SemaphoreType.DMA((len(pieces),)),
            ],
        ),
        out_shape=[
            jax.ShapeDtypeStruct((D, width), BF),
            jax.ShapeDtypeStruct((rows, D), BF),
            jax.ShapeDtypeStruct((8, D), F32),
        ],
        compiler_params=params(1),
        cost_estimate=pl.CostEstimate(
            flops=4 * rows * D * 4 * HALF + 16 * images * 6 * pad * pad * 64,
            bytes_accessed=rows * D * 16 + D * width * 4,
            transcendentals=0,
        ),
        name="attention_backward",
    )(place, *pieces, grad, qk_gain, 1.0 / qk_gain, normed, qk, v, r, pt, mixed, ff)


def norm_backward_kernel(g_ref, x_ref, mine_ref, theirs_ref, ln_ref, out_ref):
    x = x_ref[...].astype(F32)
    centred = x - jnp.mean(x, axis=-1, keepdims=True)
    rstd = lax.rsqrt(jnp.mean(centred * centred, axis=-1, keepdims=True) + EPSILON)
    shaped = centred * rstd
    scaled = (mine_ref[...].astype(F32) + theirs_ref[...].astype(F32)) * ln_ref[...]
    d_x = rstd * (
        scaled
        - jnp.mean(scaled, axis=-1, keepdims=True)
        - shaped * jnp.mean(scaled * shaped, axis=-1, keepdims=True)
    )
    out_ref[...] = (g_ref[...].astype(F32) + d_x).astype(BF)


def norm_backward(grad, x, mine, theirs, ln_gain):
    rows = x.shape[0]
    block = pl.BlockSpec((rows // 4, D), lambda i: (i, 0))
    return pl.pallas_call(
        norm_backward_kernel,
        grid=(4,),
        in_specs=[block] * 4 + [pl.BlockSpec((1, D), lambda i: (0, 0))],
        out_specs=block,
        out_shape=jax.ShapeDtypeStruct((rows, D), BF),
        compiler_params=params(1),
        cost_estimate=pl.CostEstimate(flops=12 * rows * D, bytes_accessed=rows * D * 10, transcendentals=0),
        name="norm_backward",
    )(grad, x, mine, theirs, ln_gain)


def pad_of(tokens):
    return -(-tokens // 16) * 16


def relative(value, step):
    count = lax.axis_size("dp")
    return lax.ppermute(value, "dp", [(source, source ^ step) for source in range(count)])


def after(value, *others):
    return lax.optimization_barrier((value,) + others)[0]


def gather_far(shard):
    count = lax.axis_size("dp")
    return [shard] + [relative(shard, 4 * far) for far in range(1, count // 4)]


def gather_near(quads):
    nears = [relative(piece, 2) for piece in quads]
    pieces = []
    for left, right in zip(quads, nears):
        pieces += [left, relative(left, 1), right, relative(right, 1)]
    rows, width = pieces[0].shape
    if rows % 16 == 0:
        return pieces
    me = lax.axis_index("dp")
    whole = jnp.zeros((len(pieces), rows, width), BF)
    for step, piece in enumerate(pieces):
        whole = lax.dynamic_update_slice(whole, piece[None], (me ^ step, 0, 0))
    return [whole.reshape(len(pieces) * rows, width)]


def add_low(left, right):
    return (left.astype(F32) + right.astype(F32)).astype(BF)


def pick(value, at, axis):
    return lax.dynamic_index_in_dim(value, at, axis, keepdims=False)


def coordinates():
    me = lax.axis_index("dp")
    return me % 2, (me // 2) % 2, me // 4


def scatter_core(terms):
    count = lax.axis_size("dp")
    core, _, _ = coordinates()
    rows, width = terms.shape
    shaped = terms.reshape(count // 4, 2, 2, rows // count, width)
    return pick(shaped, core, 2), pick(shaped, 1 - core, 2)


def scatter_near(total):
    _, near, _ = coordinates()
    return pick(total, near, 1), pick(total, 1 - near, 1)


def scatter_far(total):
    count = lax.axis_size("dp")
    _, _, far = coordinates()
    terms = [pick(total, far, 0)]
    for step in range(1, count // 4):
        terms.append(relative(pick(total, far ^ step, 0), 4 * step))
    return terms


def add_all(terms):
    result = terms[0].astype(F32)
    for term in terms[1:]:
        result = result + term.astype(F32)
    return result


def on_device(images, cotangent, w_qkv, w_up, w_proj, w_down, ln_gain, q_gain, k_gain):
    count = lax.axis_size("dp")
    section = lax.axis_index("section")
    first = section == 0
    me = lax.axis_index("dp")
    number, tokens, _ = images.shape
    pad = pad_of(tokens)
    rows = w_qkv.shape[1]
    group = w_down.shape[1] // 4
    units = w_up.shape[2] // 2

    def swap(value):
        return lax.ppermute(value, "section", [(0, 1), (1, 0)])

    def give(value, source):
        return lax.ppermute(value, "section", [(source, 1 - source)])

    place = jnp.stack([section, 0 * me]).astype(jnp.int32)

    def attention_half(half):
        parts = [w_proj[0]]
        for pair in range(3):
            at = pair * D + half * HALF
            parts.append(w_qkv[0, :, at : at + HALF])
        return jnp.concatenate(parts, axis=1)

    def feed_half(half):
        ups = w_up[0].reshape(rows, count, 4, group)
        parts = []
        for part in (2 * half, 2 * half + 1):
            parts.append(ups[:, :, part].reshape(rows, count * group))
        for part in (2 * half, 2 * half + 1):
            parts.append(w_down[0, part * group : (part + 1) * group])
        return jnp.concatenate(parts, axis=1)

    shards = [[None, None], [None, None]]
    held = None
    for kind, half_of in enumerate((attention_half, feed_half)):
        halves = (half_of(0), half_of(1))
        mine = jnp.where(first, halves[0], halves[1])
        theirs = jnp.where(first, halves[1], halves[0])
        other = swap(theirs if held is None else after(theirs, held))
        held = other
        shards[0][kind] = jnp.where(first, mine, other)
        shards[1][kind] = jnp.where(first, other, mine)

    own_gains = jnp.concatenate([ln_gain, q_gain, k_gain], axis=0)
    their_gains = swap(after(own_gains, *shards[0]))
    gains = (jnp.where(first, own_gains, their_gains), jnp.where(first, their_gains, own_gains))

    at_half = lambda gain: lax.dynamic_slice_in_dim(gain, section * HALF, HALF, 0)
    ln_gains = [gains[block][:1] for block in range(2)]
    qk_gains = [
        jnp.concatenate([at_half(gains[block][1]), at_half(gains[block][2])])[None] for block in range(2)
    ]

    def padded(value):
        return jnp.pad(value, ((0, 0), (0, pad - tokens), (0, 0))).reshape(number * pad, D)

    def trimmed(value):
        return value.reshape(number, pad, D)[:, :tokens]

    weights = []
    for block in range(2):
        shard = jnp.concatenate(shards[block], axis=1)
        if block == 1:
            shard = after(shard, weights[0][0])
        weights.append([lax.all_gather(shard, "dp", axis=0, tiled=True)])

    inputs, kept, parts = [padded(images)], [], []
    for block in range(2):
        saved = attention_forward(
            tokens, place, inputs[block], weights[block], ln_gains[block], qk_gains[block]
        )
        hidden, slope, part = feed_forward(place, units, saved[0], weights[block], saved[6])
        kept.append(tuple(saved[:6]) + (hidden, slope))
        parts.append(part)
        if block == 0:
            inputs.append((inputs[0].astype(F32) + part.astype(F32) + swap(part).astype(F32)).astype(BF))

    def feed_step(block, grad):
        normed, hidden, slope = kept[block][0], kept[block][6], kept[block][7]
        return feed_backward(place, units, grad, normed, weights[block], hidden, slope)

    def attention_step(block, grad, feed_part):
        return attention_backward(
            tokens, place, grad, weights[block], qk_gains[block], *kept[block][:6], feed_part
        )

    def core_stage(terms):
        mine, sent = scatter_core(terms)
        return mine, relative(sent, 1)

    def near_stage(mine, arrived):
        mine, sent = scatter_near(add_low(mine, arrived))
        return mine, sent, relative(sent, 2)

    grad = padded(cotangent)
    feed_grads, feed_part = feed_step(1, grad)
    attention_grads, part, sums_1 = attention_step(1, grad, feed_part)
    theirs = swap(part)
    terms = jnp.concatenate([attention_grads, feed_grads], axis=1)
    second_sum = lax.psum_scatter(terms, "dp", scatter_dimension=0, tiled=True).astype(F32)
    middle_grad = norm_backward(grad, inputs[1], part, theirs, ln_gains[1])
    feed_grads, feed_part = feed_step(0, middle_grad)

    feed_near = near_stage(*core_stage(feed_grads))
    attention_grads, part, sums_0 = attention_step(0, after(middle_grad, feed_near[1]), feed_part)
    feed_far = add_low(feed_near[0], feed_near[2])
    feed_terms = scatter_far(feed_far)

    gain_rows = []
    for block, sums in enumerate((sums_0, sums_1)):
        zero = jnp.zeros((D,), F32)
        put = lambda value: lax.dynamic_update_slice_in_dim(zero, value, section * HALF, 0)
        gain_rows += [sums[0] / gains[block][0], put(sums[1, :HALF]), put(sums[1, HALF:])]
    totals = jnp.stack(gain_rows)

    kept_rows, arrived = core_stage(after(attention_grads, feed_far))
    totals = totals + relative(after(totals, feed_far), 1)
    kept_rows, sent_rows, arrived = near_stage(after(kept_rows, totals), arrived)
    totals = totals + relative(after(totals, sent_rows), 2)
    attention_far = add_low(after(kept_rows, totals), arrived)
    attention_terms = scatter_far(attention_far)
    after_far = after(totals, attention_far)
    totals = add_all([totals] + [relative(after_far, 4 * far) for far in range(1, count // 4)])
    feed_sum = add_all([after(feed_terms[0], attention_far)] + feed_terms[1:])
    attention_sum = add_all([after(attention_terms[0], feed_sum, totals)] + attention_terms[1:])
    theirs = give(after(part, sent_rows), 1)
    summed = [jnp.concatenate([attention_sum, feed_sum], axis=1), second_sum]
    first_grad = norm_backward(middle_grad, inputs[0], part, theirs, ln_gains[0])
    input_grads = trimmed(jnp.where(first, first_grad, middle_grad))
    last = (inputs[1].astype(F32) + parts[1].astype(F32)) + give(parts[1], 0).astype(F32)
    outputs = trimmed(jnp.where(first, inputs[1], last.astype(BF)))

    own = jnp.where(first, summed[0], summed[1])
    theirs = swap(jnp.where(first, summed[1], summed[0]).astype(BF)).astype(F32)
    low_half = jnp.where(first, own, theirs)
    high_half = jnp.where(first, theirs, own)
    grad_proj = own[:, :D] + theirs[:, :D]
    pieces = []
    for pair in range(3):
        at = slice(D + pair * HALF, D + (pair + 1) * HALF)
        pieces += [low_half[:, at], high_half[:, at]]
    grad_qkv = jnp.concatenate(pieces, axis=1)
    ups, downs = [], []
    for source in (low_half, high_half):
        for part in range(2):
            at = SPLIT + part * D
            ups.append(source[:, at : at + D].reshape(rows, count, 1, group))
            at = SPLIT + units + part * D
            downs.append(source[:, at : at + D])
    grad_up = jnp.concatenate(ups, axis=2).reshape(rows, 2 * units)
    grad_down = jnp.concatenate(downs, axis=0)

    totals = totals + swap(after(totals, own))
    totals = jnp.where(first, totals[:3], totals[3:])
    return (
        outputs[None],
        input_grads[None],
        grad_qkv[None],
        grad_up[None],
        grad_proj[None],
        grad_down[None],
        totals[0:1],
        totals[1:2],
        totals[2:3],
    )


def solution(mesh):
    placed = (
        P("dp", None, None),
        P("dp", None, None),
        P("section", "dp", None),
        P("section", "dp", None),
        P("section", "dp", None),
        P("section", "dp", None),
        P("section", None),
        P("section", None),
        P("section", None),
    )
    return jax.shard_map(
        on_device,
        mesh=mesh,
        in_specs=placed,
        out_specs=(
            P("section", "dp", None, None),
            P("section", "dp", None, None),
            P("section", "dp", None),
            P("section", "dp", None),
            P("section", "dp", None),
            P("section", "dp", None),
            P("section", None),
            P("section", None),
            P("section", None),
        ),
        check_vma=False,
    )
```

```python
from functools import partial

import jax
import jax.numpy as jnp
from jax import lax
from jax.experimental import pallas as pl
from jax.experimental.pallas import tpu as pltpu
from jax.sharding import PartitionSpec as P

D = 768
HEADS = 12
HEAD = 64
HALF = D // 2
PAIRS = HALF // 128
EPSILON = 1e-06
TILE = 256
BF = jnp.bfloat16
F32 = jnp.float32
SPLIT = D + 3 * HALF
ANYWHERE = pl.BlockSpec(memory_space=pl.ANY)
C0 = 0.7978845608028654
C1 = 0.044715


def dot(a, b):
    return lax.dot_general(a, b, (((1,), (0,)), ((), ())), preferred_element_type=F32)


def dot_nt(a, b):
    return lax.dot_general(a, b, (((1,), (1,)), ((), ())), preferred_element_type=F32)


def dot_tn(a, b):
    return lax.dot_general(a, b, (((0,), (0,)), ((), ())), preferred_element_type=F32)


def head_means(x):
    row = lax.broadcasted_iota(jnp.int32, (256, 256), 0) // HEAD
    col = lax.broadcasted_iota(jnp.int32, (256, 256), 1) // HEAD
    ones = jnp.where(row == col, 1.0 / HEAD, 0.0).astype(BF)
    high = x.astype(BF)
    rest = (x - high.astype(F32)).astype(BF)
    parts = []
    for at in range(0, x.shape[1], 256):
        parts.append(dot(high[:, at : at + 256], ones) + dot(rest[:, at : at + 256], ones))
    return jnp.concatenate(parts, axis=1)


def half_mask(rows, h):
    return lax.broadcasted_iota(jnp.int32, (rows, 128), 1) // HEAD == h


def params(steps, megabytes=20):
    return pltpu.CompilerParams(
        dimension_semantics=("arbitrary",) * steps, vmem_limit_bytes=megabytes * 1024 * 1024
    )


def copies(place, pieces, columns, dest_ref, sems):
    made = []
    for step, piece in enumerate(pieces):
        rows = piece.shape[0]
        at = pl.ds(pl.multiple_of((place[1] ^ step) * rows, rows), rows)
        made.append(pltpu.make_async_copy(piece.at[:, columns], dest_ref.at[at, :], sems.at[step]))
    return made


def attention_forward_kernel(tokens, count, place, *refs):
    pieces = refs[:count]
    (
        x_ref,
        ln_ref,
        gain_ref,
        normed_ref,
        qk_ref,
        v_ref,
        r_ref,
        pt_ref,
        mixed_ref,
        part_ref,
        w_ref,
        sems,
    ) = refs[count:]
    section = place[0]

    @pl.when(pl.program_id(0) == 0)
    def _():
        for copy in copies(place, pieces, slice(0, SPLIT), w_ref, sems):
            copy.start()

    x = x_ref[...].astype(F32)
    rows = x.shape[0]
    pad = rows // 2
    centred = x - jnp.mean(x, axis=-1, keepdims=True)
    spread = jnp.mean(centred * centred, axis=-1, keepdims=True)
    normed = (centred * lax.rsqrt(spread + EPSILON) * ln_ref[...]).astype(BF)
    normed_ref[...] = normed

    @pl.when(pl.program_id(0) == 0)
    def _():
        for copy in copies(place, pieces, slice(0, SPLIT), w_ref, sems):
            copy.wait()

    qkv = dot(normed, w_ref[:, D:])
    qk = qkv[:, :D]
    centred = qk - head_means(qk)
    rstd = lax.rsqrt(head_means(centred * centred) + EPSILON)
    qk_ref[...] = (centred * rstd * gain_ref[...]).astype(BF)
    r_ref[...] = rstd.astype(BF)
    v_ref[...] = qkv[:, D:].astype(BF)
    valid = lax.broadcasted_iota(jnp.int32, (pad, pad), 0) < tokens
    for image in range(2):
        at = slice(image * pad, (image + 1) * pad)
        for pair in range(PAIRS):
            query = qk_ref[at, pair * 128 : (pair + 1) * 128]
            key = qk_ref[at, HALF + pair * 128 : HALF + (pair + 1) * 128]
            value = v_ref[at, pair * 128 : (pair + 1) * 128]
            mixed = jnp.zeros((pad, 128), F32)
            for h in range(2):
                mask = half_mask(pad, h)
                scores = dot_nt(jnp.where(mask, key, 0), query) * HEAD ** (-0.5)
                scores = jnp.where(valid, scores, -1e30)
                top = jnp.max(scores, axis=0, keepdims=True)
                weights = jnp.exp(scores - top)
                probs = weights * (1.0 / jnp.sum(weights, axis=0, keepdims=True))
                probs = probs.astype(BF)
                pt_ref[image, 2 * pair + h] = probs
                mixed += dot_tn(probs, jnp.where(mask, value, 0))
            mixed_ref[at, pair * 128 : (pair + 1) * 128] = mixed.astype(BF)
    proj = w_ref[pl.ds(pl.multiple_of(section * HALF, HALF), HALF), :D]
    part_ref[...] = dot(mixed_ref[...], proj).astype(BF)


def attention_forward(tokens, place, x, pieces, ln_gain, qk_gain):
    rows = x.shape[0]
    images = rows // pad_of(tokens)
    pad = pad_of(tokens)
    step = 2 * pad
    row = lambda width: pl.BlockSpec((step, width), lambda i, s: (i, 0))
    full = lambda shape: pl.BlockSpec(shape, lambda i, s: (0, 0), pipeline_mode=pl.Buffered(1))
    return pl.pallas_call(
        partial(attention_forward_kernel, tokens, len(pieces)),
        grid_spec=pltpu.PrefetchScalarGridSpec(
            num_scalar_prefetch=1,
            grid=(images // 2,),
            in_specs=[ANYWHERE] * len(pieces) + [row(D), full((1, D)), full((1, D))],
            out_specs=[
                row(D),
                row(D),
                row(HALF),
                row(D),
                pl.BlockSpec((2, 2 * PAIRS, pad, pad), lambda i, s: (i, 0, 0, 0)),
                row(HALF),
                row(D),
            ],
            scratch_shapes=[
                pltpu.VMEM((D, SPLIT), BF),
                pltpu.SemaphoreType.DMA((len(pieces),)),
            ],
        ),
        out_shape=[
            jax.ShapeDtypeStruct((rows, D), BF),
            jax.ShapeDtypeStruct((rows, D), BF),
            jax.ShapeDtypeStruct((rows, HALF), BF),
            jax.ShapeDtypeStruct((rows, D), BF),
            jax.ShapeDtypeStruct((images, 2 * PAIRS, pad, pad), BF),
            jax.ShapeDtypeStruct((rows, HALF), BF),
            jax.ShapeDtypeStruct((rows, D), BF),
        ],
        compiler_params=params(1),
        cost_estimate=pl.CostEstimate(
            flops=2 * rows * D * (3 * HALF + HALF) + 8 * images * 6 * pad * pad * 64,
            bytes_accessed=rows * D * 12 + D * 1920 * 2,
            transcendentals=images * 6 * pad * pad,
        ),
        name="attention_forward",
    )(place, *pieces, x, ln_gain, qk_gain)


def feed_copies(place, pieces, units, up_ref, down_ref, sems):
    base = pieces[0].shape[1] - 2 * units
    ups = copies(place, pieces, slice(base, base + units), up_ref, sems.at[0])
    downs = []
    for part in range(units // D):
        columns = slice(base + units + part * D, base + units + (part + 1) * D)
        downs += copies(place, pieces, columns, down_ref.at[part], sems.at[1 + part])
    return ups, downs


def feed_tiles(step):
    across = D // TILE
    columns = pl.ds(pl.multiple_of(step * TILE, TILE), TILE)
    return columns, step // across, pl.ds(pl.multiple_of((step % across) * TILE, TILE), TILE)


def feed_forward_kernel(steps, count, place, *refs):
    pieces = refs[:count]
    normed_ref, part_ref, hidden_ref, slope_ref, out_ref, acc_ref, up_ref, down_ref, sems = refs[count:]
    step = pl.program_id(0)
    columns, part, rows = feed_tiles(step)

    @pl.when(step == 0)
    def _():
        ups, downs = feed_copies(place, pieces, steps * TILE, up_ref, down_ref, sems)
        for copy in ups + downs:
            copy.start()
        for copy in ups + downs:
            copy.wait()

    up = dot(normed_ref[...], up_ref[:, columns])
    square = up * up
    tanh = jnp.tanh(C0 * up * (1.0 + C1 * square))
    hidden = (0.5 * up * (1.0 + tanh)).astype(BF)
    slope = 0.5 * (1.0 + tanh) + (0.5 * C0) * up * (1.0 - tanh * tanh) * (1.0 + (3.0 * C1) * square)
    hidden_ref[...] = hidden
    slope_ref[...] = slope.astype(BF)
    term = dot(hidden, down_ref[part, rows, :])

    @pl.when(step == 0)
    def _():
        acc_ref[...] = part_ref[...].astype(F32) + term

    @pl.when(step > 0)
    def _():
        acc_ref[...] += term

    @pl.when(step == steps - 1)
    def _():
        out_ref[...] = acc_ref[...].astype(BF)


def feed_scratch(rows, units, count):
    return [
        pltpu.VMEM((rows, D), F32),
        pltpu.VMEM((D, units), BF),
        pltpu.VMEM((units // D, D, D), BF),
        pltpu.SemaphoreType.DMA((1 + units // D, count)),
    ]


def feed_forward(place, units, normed, pieces, part):
    rows = normed.shape[0]
    steps = units // TILE
    whole = pl.BlockSpec((rows, D), lambda j, s: (0, 0))
    tile = pl.BlockSpec((rows, TILE), lambda j, s: (0, j))
    return pl.pallas_call(
        partial(feed_forward_kernel, steps, len(pieces)),
        grid_spec=pltpu.PrefetchScalarGridSpec(
            num_scalar_prefetch=1,
            grid=(steps,),
            in_specs=[ANYWHERE] * len(pieces) + [whole, whole],
            out_specs=[tile, tile, whole],
            scratch_shapes=feed_scratch(rows, units, len(pieces)),
        ),
        out_shape=[
            jax.ShapeDtypeStruct((rows, units), BF),
            jax.ShapeDtypeStruct((rows, units), BF),
            jax.ShapeDtypeStruct((rows, D), BF),
        ],
        compiler_params=params(1),
        cost_estimate=pl.CostEstimate(
            flops=4 * rows * D * units,
            bytes_accessed=rows * D * 6 + rows * units * 4 + D * units * 4,
            transcendentals=rows * units,
        ),
        name="feed_forward",
    )(place, *pieces, normed, part)


def feed_backward_kernel(steps, count, place, *refs):
    pieces = refs[:count]
    g_ref, normed_ref, hidden_ref, slope_ref, grad_ref, out_ref, acc_ref, up_ref, down_ref, sems = refs[count:]
    step = pl.program_id(0)
    columns, part, rows = feed_tiles(step)

    @pl.when(step == 0)
    def _():
        ups, downs = feed_copies(place, pieces, steps * TILE, up_ref, down_ref, sems)
        for copy in downs + ups:
            copy.start()
        for copy in downs + ups:
            copy.wait()

    grad = g_ref[...]
    d_up = (slope_ref[...].astype(F32) * dot_nt(grad, down_ref[part, rows, :])).astype(BF)
    there = pl.ds(pl.multiple_of(steps * TILE + part * D, D), D)
    grad_ref[rows, there] = dot_tn(hidden_ref[...], grad).astype(BF)
    grad_ref[:, columns] = dot_tn(normed_ref[...], d_up).astype(BF)
    term = dot_nt(d_up, up_ref[:, columns])

    @pl.when(step == 0)
    def _():
        acc_ref[...] = term

    @pl.when(step > 0)
    def _():
        acc_ref[...] += term

    @pl.when(step == steps - 1)
    def _():
        out_ref[...] = acc_ref[...].astype(BF)


def feed_backward(place, units, grad, normed, pieces, hidden, slope):
    rows = normed.shape[0]
    steps = units // TILE
    whole = pl.BlockSpec((rows, D), lambda j, s: (0, 0))
    tile = pl.BlockSpec((rows, TILE), lambda j, s: (0, j))
    return pl.pallas_call(
        partial(feed_backward_kernel, steps, len(pieces)),
        grid_spec=pltpu.PrefetchScalarGridSpec(
            num_scalar_prefetch=1,
            grid=(steps,),
            in_specs=[ANYWHERE] * len(pieces) + [whole, whole, tile, tile],
            out_specs=[pl.BlockSpec((D, 2 * units), lambda j, s: (0, 0)), whole],
            scratch_shapes=feed_scratch(rows, units, len(pieces)),
        ),
        out_shape=[
            jax.ShapeDtypeStruct((D, 2 * units), BF),
            jax.ShapeDtypeStruct((rows, D), BF),
        ],
        compiler_params=params(1),
        cost_estimate=pl.CostEstimate(
            flops=8 * rows * D * units,
            bytes_accessed=rows * D * 6 + rows * units * 4 + D * units * 8,
            transcendentals=0,
        ),
        name="feed_backward",
    )(place, *pieces, grad, normed, hidden, slope)


def attention_backward_kernel(steps, count, place, *refs):
    pieces = refs[:count]
    (
        g_ref,
        gain_ref,
        inverse_ref,
        normed_ref,
        qk_ref,
        v_ref,
        r_ref,
        pt_ref,
        mixed_ref,
        ff_ref,
        grad_ref,
        out_ref,
        sums_ref,
        qkv_acc,
        proj_acc,
        d_qk,
        d_qkv,
        w_ref,
        sems,
    ) = refs[count:]
    step = pl.program_id(0)
    section = place[0]
    rows = g_ref.shape[0]
    pad = rows // 2

    @pl.when(step == 0)
    def _():
        for copy in copies(place, pieces, slice(0, SPLIT), w_ref, sems):
            copy.start()
        sums_ref[...] = jnp.zeros_like(sums_ref)
        for copy in copies(place, pieces, slice(0, SPLIT), w_ref, sems):
            copy.wait()

    grad = g_ref[...]
    here = pl.ds(pl.multiple_of(section * HALF, HALF), HALF)
    d_mixed = dot_nt(grad, w_ref[here, :D]).astype(BF)
    proj_term = dot_tn(mixed_ref[...], grad)
    for image in range(2):
        at = slice(image * pad, (image + 1) * pad)
        for pair in range(PAIRS):
            lanes = slice(pair * 128, (pair + 1) * 128)
            key_lanes = slice(HALF + pair * 128, HALF + (pair + 1) * 128)
            query = qk_ref[at, lanes]
            key = qk_ref[at, key_lanes]
            value = v_ref[at, lanes]
            d_mix = d_mixed[at, lanes]
            d_query = jnp.zeros((pad, 128), F32)
            d_key = jnp.zeros((pad, 128), F32)
            d_value = jnp.zeros((pad, 128), F32)
            for h in range(2):
                mask = half_mask(pad, h)
                d_mix_head = jnp.where(mask, d_mix, 0)
                probs_low = pt_ref[image, 2 * pair + h]
                probs = probs_low.astype(F32)
                d_probs = dot_nt(value, d_mix_head)
                weighted = jnp.sum(probs * d_probs, axis=0, keepdims=True)
                d_scores = (probs * (d_probs - weighted)).astype(BF)
                d_value += dot(probs_low, d_mix_head)
                d_key += dot(d_scores, jnp.where(mask, query, 0))
                d_query += dot_tn(d_scores, jnp.where(mask, key, 0))
            d_qk[at, lanes] = d_query * HEAD ** (-0.5)
            d_qk[at, key_lanes] = d_key * HEAD ** (-0.5)
            d_qkv[at, D + pair * 128 : D + (pair + 1) * 128] = d_value.astype(BF)
    d_normed_heads = d_qk[...]
    shaped = qk_ref[...].astype(F32) * inverse_ref[...]
    sums_ref[1:2, :] += jnp.sum(d_normed_heads * shaped, axis=0, keepdims=True)
    scaled = d_normed_heads * gain_ref[...]
    d_qkv[:, :D] = (
        r_ref[...].astype(F32) * (scaled - head_means(scaled) - shaped * head_means(scaled * shaped))
    ).astype(BF)
    normed = normed_ref[...]
    qkv_term = dot_tn(normed, d_qkv[...])
    d_normed = dot_nt(d_qkv[...], w_ref[:, D:]) + ff_ref[...].astype(F32)
    out_ref[...] = d_normed.astype(BF)
    sums_ref[0:1, :] += jnp.sum(d_normed * normed.astype(F32), axis=0, keepdims=True)

    @pl.when(step == 0)
    def _():
        qkv_acc[...] = qkv_term
        proj_acc[...] = proj_term

    @pl.when(step > 0)
    def _():
        qkv_acc[...] += qkv_term
        proj_acc[...] += proj_term

    @pl.when(step == steps - 1)
    def _():
        there = pl.ds(pl.multiple_of((1 - section) * HALF, HALF), HALF)
        grad_ref[here, :D] = proj_acc[...].astype(BF)
        grad_ref[there, :D] = jnp.zeros((HALF, D), BF)
        grad_ref[:, D:] = qkv_acc[...].astype(BF)


def attention_backward(tokens, place, grad, pieces, qk_gain, normed, qk, v, r, pt, mixed, ff):
    rows = normed.shape[0]
    pad = pad_of(tokens)
    images = rows // pad
    step = 2 * pad
    steps = images // 2
    width = SPLIT
    row = lambda columns: pl.BlockSpec((step, columns), lambda i, s: (i, 0))
    full = lambda shape: pl.BlockSpec(shape, lambda i, s: (0, 0), pipeline_mode=pl.Buffered(1))
    return pl.pallas_call(
        partial(attention_backward_kernel, steps, len(pieces)),
        grid_spec=pltpu.PrefetchScalarGridSpec(
            num_scalar_prefetch=1,
            grid=(steps,),
            in_specs=[ANYWHERE] * len(pieces)
            + [
                row(D),
                full((1, D)),
                full((1, D)),
                row(D),
                row(D),
                row(HALF),
                row(D),
                pl.BlockSpec((2, 2 * PAIRS, pad, pad), lambda i, s: (i, 0, 0, 0)),
                row(HALF),
                row(D),
            ],
            out_specs=[
                pl.BlockSpec((D, width), lambda i, s: (0, 0)),
                row(D),
                pl.BlockSpec((8, D), lambda i, s: (0, 0)),
            ],
            scratch_shapes=[
                pltpu.VMEM((D, 3 * HALF), F32),
                pltpu.VMEM((HALF, D), F32),
                pltpu.VMEM((step, D), F32),
                pltpu.VMEM((step, 3 * HALF), BF),
                pltpu.VMEM((D, SPLIT), BF),
                pltpu.SemaphoreType.DMA((len(pieces),)),
            ],
        ),
        out_shape=[
            jax.ShapeDtypeStruct((D, width), BF),
            jax.ShapeDtypeStruct((rows, D), BF),
            jax.ShapeDtypeStruct((8, D), F32),
        ],
        compiler_params=params(1),
        cost_estimate=pl.CostEstimate(
            flops=4 * rows * D * 4 * HALF + 16 * images * 6 * pad * pad * 64,
            bytes_accessed=rows * D * 16 + D * width * 4,
            transcendentals=0,
        ),
        name="attention_backward",
    )(place, *pieces, grad, qk_gain, 1.0 / qk_gain, normed, qk, v, r, pt, mixed, ff)


def copy_all(pairs, sems, wait):
    for at, (source, target) in enumerate(pairs):
        copy = pltpu.make_async_copy(source, target, sems.at[at])
        if wait:
            copy.wait()
        else:
            copy.start()


def weight_pairs(w_ref, units, attention_ref, up_ref, down_ref):
    pairs = [
        (w_ref.at[:, pl.ds(0, SPLIT)], attention_ref),
        (w_ref.at[:, pl.ds(SPLIT, units)], up_ref),
    ]
    for part in range(units // D):
        pairs.append((w_ref.at[:, pl.ds(SPLIT + units + part * D, D)], down_ref.at[part]))
    return pairs


def gelu(up):
    square = up * up
    tanh = jnp.tanh(up * (C0 + (C0 * C1) * square))
    share = 0.5 + 0.5 * tanh
    slope = share + up * (share * (1.0 - share)) * (2.0 * C0 + (6.0 * C0 * C1) * square)
    return (up * share).astype(BF), slope


def attend(tokens, qk_ref, v_ref, pt_ref, mixed_ref, rows):
    pad = v_ref.shape[0]
    valid = lax.broadcasted_iota(jnp.int32, (pad, pad), 0) < tokens
    for pair in range(PAIRS):
        lanes = slice(pair * 128, (pair + 1) * 128)
        query = qk_ref[:, lanes]
        key = qk_ref[:, HALF + pair * 128 : HALF + (pair + 1) * 128]
        value = v_ref[:, lanes]
        mixed = jnp.zeros((pad, 128), F32)
        for h in range(2):
            mask = half_mask(pad, h)
            scores = dot_nt(jnp.where(mask, key, 0), query) * HEAD ** (-0.5)
            scores = jnp.where(valid, scores, -1e30)
            top = jnp.max(scores, axis=0, keepdims=True)
            powers = jnp.exp(scores - top)
            probs = (powers * (1.0 / jnp.sum(powers, axis=0, keepdims=True))).astype(BF)
            pt_ref[2 * pair + h] = probs
            mixed += dot_tn(probs, jnp.where(mask, value, 0))
        mixed_ref[rows, lanes] = mixed.astype(BF)


def attend_back(query_of, key_of, value_of, probs_of, d_mixed, d_qk_ref, d_qkv_ref, rows):
    pad = d_mixed.shape[0]
    for pair in range(PAIRS):
        lanes = slice(pair * 128, (pair + 1) * 128)
        query, key, value = query_of(pair), key_of(pair), value_of(pair)
        d_mix = d_mixed[:, lanes]
        d_query = jnp.zeros((pad, 128), F32)
        d_key = jnp.zeros((pad, 128), F32)
        d_value = jnp.zeros((pad, 128), F32)
        for h in range(2):
            mask = half_mask(pad, h)
            d_mix_head = jnp.where(mask, d_mix, 0)
            probs_low = probs_of(2 * pair + h)
            probs = probs_low.astype(F32)
            d_probs = dot_nt(value, d_mix_head)
            weighted = jnp.sum(probs * d_probs, axis=0, keepdims=True)
            d_scores = (probs * (d_probs - weighted)).astype(BF)
            d_value += dot(probs_low, d_mix_head)
            d_key += dot(d_scores, jnp.where(mask, query, 0))
            d_query += dot_tn(d_scores, jnp.where(mask, key, 0))
        d_qk_ref[:, lanes] = d_query * HEAD ** (-0.5)
        d_qk_ref[:, HALF + pair * 128 : HALF + (pair + 1) * 128] = d_key * HEAD ** (-0.5)
        d_qkv_ref[rows, D + pair * 128 : D + (pair + 1) * 128] = d_value.astype(BF)


def head_norm_back(d_heads, shaped, rstd, gain):
    scaled = d_heads * gain
    return (rstd * (scaled - head_means(scaled) - shaped * head_means(scaled * shaped))).astype(BF)


def whole_block_kernel(
    tokens,
    images,
    units,
    place,
    w_ref,
    x_ref,
    g_ref,
    ln_ref,
    gain_ref,
    part_ref,
    out_ref,
    sums_ref,
    normed_hbm,
    mixed_hbm,
    hidden_hbm,
    d_up_hbm,
    d_qkv_hbm,
    attention_ref,
    up_ref,
    down_ref,
    normed_ref,
    mixed_ref,
    hidden_ref,
    d_up_ref,
    d_qkv_ref,
    qk_ref,
    v_ref,
    shaped_ref,
    rstd_ref,
    pt_ref,
    slope_ref,
    d_qk_ref,
    sems,
    out_sems,
):
    section = place[0]
    pairs = weight_pairs(w_ref, units, attention_ref, up_ref, down_ref)
    copy_all(pairs, sems, False)
    sums_ref[...] = jnp.zeros_like(sums_ref)
    pad = x_ref.shape[0] // images
    here = pl.ds(pl.multiple_of(section * HALF, HALF), HALF)

    def leaving(image):
        rows = pl.ds(pl.multiple_of(image * pad, pad), pad)
        made = []
        for source, target in (
            (normed_ref, normed_hbm),
            (mixed_ref, mixed_hbm),
            (hidden_ref, hidden_hbm),
            (d_up_ref, d_up_hbm),
            (d_qkv_ref, d_qkv_hbm),
        ):
            made.append((source.at[rows, :], target.at[rows, :]))
        return made

    copy_all(pairs, sems, True)

    def image_step(image, carry):
        rows = pl.ds(pl.multiple_of(image * pad, pad), pad)
        x = x_ref[rows, :].astype(F32)
        centred = x - jnp.mean(x, axis=-1, keepdims=True)
        spread = jnp.mean(centred * centred, axis=-1, keepdims=True)
        normed = (centred * lax.rsqrt(spread + EPSILON) * ln_ref[...]).astype(BF)
        normed_ref[rows, :] = normed
        qkv = dot(normed, attention_ref[:, D:])
        qk = qkv[:, :D]
        centred = qk - head_means(qk)
        rstd = lax.rsqrt(head_means(centred * centred) + EPSILON)
        rstd_ref[...] = rstd
        shaped = centred * rstd
        shaped_ref[...] = shaped
        qk_ref[...] = (shaped * gain_ref[...]).astype(BF)
        v_ref[...] = qkv[:, D:].astype(BF)
        attend(tokens, qk_ref, v_ref, pt_ref, mixed_ref, rows)
        part = dot(mixed_ref[rows, :], attention_ref[here, :D])
        grad = g_ref[rows, :]
        hidden, slope = gelu(dot(normed, up_ref[...]))
        hidden_ref[rows, :] = hidden
        slope_ref[...] = slope
        for at in range(units // D):
            columns = slice(at * D, (at + 1) * D)
            part += dot(hidden[:, columns], down_ref[at])
            d_up_ref[rows, columns] = (slope_ref[:, columns] * dot_nt(grad, down_ref[at])).astype(BF)
        part_ref[rows, :] = part.astype(BF)
        d_normed = dot_nt(d_up_ref[rows, :], up_ref[...])
        d_mixed = dot_nt(grad, attention_ref[here, :D]).astype(BF)
        attend_back(
            lambda pair: qk_ref[:, pair * 128 : (pair + 1) * 128],
            lambda pair: qk_ref[:, HALF + pair * 128 : HALF + (pair + 1) * 128],
            lambda pair: v_ref[:, pair * 128 : (pair + 1) * 128],
            lambda head: pt_ref[head],
            d_mixed,
            d_qk_ref,
            d_qkv_ref,
            rows,
        )
        d_heads = d_qk_ref[...]
        shaped = shaped_ref[...]
        sums_ref[1:2, :] += jnp.sum(d_heads * shaped, axis=0, keepdims=True)
        d_qkv_ref[rows, :D] = head_norm_back(d_heads, shaped, rstd_ref[...], gain_ref[...])
        d_normed += dot_nt(d_qkv_ref[rows, :], attention_ref[:, D:])
        out_ref[rows, :] = d_normed.astype(BF)
        sums_ref[0:1, :] += jnp.sum(d_normed * normed_ref[rows, :].astype(F32), axis=0, keepdims=True)
        copy_all(leaving(image), out_sems.at[image], False)
        return carry

    lax.fori_loop(0, images, image_step, 0)
    for image in range(images):
        copy_all(leaving(image), out_sems.at[image], True)


def weight_grads_kernel(units, halves, place, *refs):
    sources = [refs[6 * half : 6 * half + 6] for half in range(halves)]
    grad_ref, hidden_ref, g_ref, normed_ref, d_up_ref, mixed_ref, d_qkv_ref, stage_ref, sems, out_sems = refs[6 * halves :]
    targets = (hidden_ref, g_ref, normed_ref, d_up_ref, mixed_ref, d_qkv_ref)
    pairs = []
    for half in range(halves):
        rows = sources[half][0].shape[0]
        at = pl.ds(half * rows, rows)
        pairs.append([(source, target.at[at, :]) for source, target in zip(sources[half], targets)])
    for half in range(halves):
        copy_all(pairs[half], sems.at[half], False)
    for half in range(halves):
        copy_all(pairs[half], sems.at[half], True)
    section = place[0]
    made = []
    for at, columns in enumerate((pl.ds(SPLIT, 2 * units), pl.ds(0, SPLIT))):
        if at == 0:
            feed_grads(units, g_ref, normed_ref, hidden_ref, d_up_ref, stage_ref, SPLIT)
        else:
            attention_grads(section, g_ref, normed_ref, mixed_ref, d_qkv_ref, stage_ref)
        made.append(
            pltpu.make_async_copy(stage_ref.at[:, columns], grad_ref.at[:, columns], out_sems.at[at])
        )
        made[-1].start()
    for copy in made:
        copy.wait()


def weight_grads(place, units, halves):
    rows = sum(half[0].shape[0] for half in halves)
    return pl.pallas_call(
        partial(weight_grads_kernel, units, len(halves)),
        grid_spec=pltpu.PrefetchScalarGridSpec(
            num_scalar_prefetch=1,
            grid=(1,),
            in_specs=[ANYWHERE] * (6 * len(halves)),
            out_specs=ANYWHERE,
            scratch_shapes=[
                pltpu.VMEM((rows, units), BF),
                pltpu.VMEM((rows, D), BF),
                pltpu.VMEM((rows, D), BF),
                pltpu.VMEM((rows, units), BF),
                pltpu.VMEM((rows, HALF), BF),
                pltpu.VMEM((rows, 3 * HALF), BF),
                pltpu.VMEM((D, SPLIT + 2 * units), BF),
                pltpu.SemaphoreType.DMA((len(halves), 6)),
                pltpu.SemaphoreType.DMA((2,)),
            ],
        ),
        out_shape=jax.ShapeDtypeStruct((D, SPLIT + 2 * units), BF),
        compiler_params=params(1, 36),
        cost_estimate=pl.CostEstimate(
            flops=2 * rows * D * (4 * HALF + 2 * units),
            bytes_accessed=rows * (2 * units + 6 * HALF + 2 * D) * 2 + D * (SPLIT + 2 * units) * 2,
            transcendentals=0,
        ),
        name="weight_grads",
    )(place, *[value for half in halves for value in half])


def copy_all_from(pairs, first, sems):
    for at in range(first, len(pairs)):
        pltpu.make_async_copy(pairs[at][0], pairs[at][1], sems.at[at]).wait()


def feed_grads(units, g_ref, normed_ref, hidden_ref, d_up_ref, stage_ref, base):
    for at in range(0, units, 512):
        stage_ref[:, base + at : base + at + 512] = dot_tn(normed_ref[...], d_up_ref[:, at : at + 512]).astype(BF)
    for at in range(0, units, 384):
        rows = slice(at % D, at % D + 384)
        columns = slice(base + units + at // D * D, base + units + at // D * D + D)
        stage_ref[rows, columns] = dot_tn(hidden_ref[:, at : at + 384], g_ref[...]).astype(BF)


def attention_grads(section, g_ref, normed_ref, mixed_ref, d_qkv_ref, stage_ref):
    here = pl.ds(pl.multiple_of(section * HALF, HALF), HALF)
    there = pl.ds(pl.multiple_of((1 - section) * HALF, HALF), HALF)
    stage_ref[here, :D] = dot_tn(mixed_ref[...], g_ref[...]).astype(BF)
    stage_ref[there, :D] = jnp.zeros((HALF, D), BF)
    for at in range(0, 3 * HALF, 384):
        stage_ref[:, D + at : D + at + 384] = dot_tn(normed_ref[...], d_qkv_ref[:, at : at + 384]).astype(BF)


def whole_block(tokens, units, place, x, grad, weights, ln_gain, qk_gain, half, halves):
    rows = x.shape[0] // halves
    pad = pad_of(tokens)
    images = rows // pad
    full = lambda shape: pl.BlockSpec(shape, lambda i, s: (0, 0))
    own = pl.BlockSpec((rows, D), lambda i, s: (half, 0))
    widths = (D, HALF, units, units, 3 * HALF)
    return pl.pallas_call(
        partial(whole_block_kernel, tokens, images, units),
        grid_spec=pltpu.PrefetchScalarGridSpec(
            num_scalar_prefetch=1,
            grid=(1,),
            in_specs=[ANYWHERE, own, own, full((1, D)), full((1, D))],
            out_specs=[full((rows, D)), full((rows, D)), full((8, D))] + [ANYWHERE] * 5,
            scratch_shapes=[
                pltpu.VMEM((D, SPLIT), BF),
                pltpu.VMEM((D, units), BF),
                pltpu.VMEM((units // D, D, D), BF),
            ]
            + [pltpu.VMEM((rows, width), BF) for width in widths]
            + [
                pltpu.VMEM((pad, D), BF),
                pltpu.VMEM((pad, HALF), BF),
                pltpu.VMEM((pad, D), F32),
                pltpu.VMEM((pad, D), F32),
                pltpu.VMEM((2 * PAIRS, pad, pad), BF),
                pltpu.VMEM((pad, units), F32),
                pltpu.VMEM((pad, D), F32),
                pltpu.SemaphoreType.DMA((2 + units // D,)),
                pltpu.SemaphoreType.DMA((images, 5)),
            ],
        ),
        out_shape=[
            jax.ShapeDtypeStruct((rows, D), BF),
            jax.ShapeDtypeStruct((rows, D), BF),
            jax.ShapeDtypeStruct((8, D), F32),
        ]
        + [jax.ShapeDtypeStruct((rows, width), BF) for width in widths],
        compiler_params=params(1, 36),
        cost_estimate=pl.CostEstimate(
            flops=4 * rows * D * (4 * HALF + 2 * units),
            bytes_accessed=rows * D * 20 + D * (SPLIT + 2 * units) * 2,
            transcendentals=rows * units,
        ),
        name="whole_block",
    )(place, weights, x, grad, ln_gain, qk_gain)


def spread(place, count, stage_ref, columns, mine_ref, sent_ref, sems):
    core, near, far = place[1], place[2], place[3]
    rows = stage_ref.shape[0] // count
    made = []
    for which, target in enumerate((sent_ref, mine_ref)):
        for at in range(count // 2):
            other, step = at // (count // 4), at % (count // 4)
            device = (far ^ step) * 4 + (near ^ other) * 2 + (core if which else 1 - core)
            source = stage_ref.at[pl.ds(pl.multiple_of(device * rows, rows), rows), columns]
            made.append(
                pltpu.make_async_copy(
                    source, target.at[pl.ds(at * rows, rows), columns], sems.at[which * (count // 2) + at]
                )
            )
    return made


def feed_back_kernel(
    images,
    units,
    count,
    place,
    w_ref,
    g_hbm,
    normed_hbm,
    hidden_hbm,
    slope_hbm,
    out_ref,
    mine_ref,
    sent_ref,
    up_ref,
    down_ref,
    g_ref,
    normed_ref,
    hidden_ref,
    slope_ref,
    d_up_ref,
    stage_ref,
    sems,
    out_sems,
):
    pairs = []
    for part in range(units // D):
        pairs.append((w_ref.at[:, pl.ds(SPLIT + units + part * D, D)], down_ref.at[part]))
    pairs += [
        (g_hbm, g_ref),
        (slope_hbm, slope_ref),
        (w_ref.at[:, pl.ds(SPLIT, units)], up_ref),
        (hidden_hbm, hidden_ref),
        (normed_hbm, normed_ref),
    ]
    ready = len(pairs) - 2
    copy_all(pairs, sems, False)
    copy_all(pairs[:ready], sems, True)
    pad = g_ref.shape[0] // images

    def image_step(image, carry):
        rows = pl.ds(pl.multiple_of(image * pad, pad), pad)
        grad = g_ref[rows, :]
        for at in range(units // D):
            columns = slice(at * D, (at + 1) * D)
            d_up_ref[rows, columns] = (
                slope_ref[rows, columns].astype(F32) * dot_nt(grad, down_ref[at])
            ).astype(BF)
        out_ref[rows, :] = dot_nt(d_up_ref[rows, :], up_ref[...]).astype(BF)
        return carry

    lax.fori_loop(0, images, image_step, 0)
    copy_all_from(pairs, ready, sems)
    for at in range(0, units, 384):
        rows = slice(at % D, at % D + 384)
        columns = slice(units + at // D * D, units + at // D * D + D)
        stage_ref[rows, columns] = dot_tn(hidden_ref[:, at : at + 384], g_ref[...]).astype(BF)
    downs = spread(place, count, stage_ref, pl.ds(units, units), mine_ref, sent_ref, out_sems.at[0])
    for copy in downs:
        copy.start()
    for at in range(0, units, 512):
        stage_ref[:, at : at + 512] = dot_tn(normed_ref[...], d_up_ref[:, at : at + 512]).astype(BF)
    ups = spread(place, count, stage_ref, pl.ds(0, units), mine_ref, sent_ref, out_sems.at[1])
    for copy in ups:
        copy.start()
    for copy in downs + ups:
        copy.wait()


def feed_back(place, units, count, grad, weights, normed, hidden, slope):
    rows = normed.shape[0]
    images = 4 if rows % 64 == 0 else 1
    sends = D // 2
    return pl.pallas_call(
        partial(feed_back_kernel, images, units, count),
        grid_spec=pltpu.PrefetchScalarGridSpec(
            num_scalar_prefetch=1,
            grid=(1,),
            in_specs=[ANYWHERE] * 5,
            out_specs=[pl.BlockSpec((rows, D), lambda i, s: (0, 0)), ANYWHERE, ANYWHERE],
            scratch_shapes=[
                pltpu.VMEM((D, units), BF),
                pltpu.VMEM((units // D, D, D), BF),
                pltpu.VMEM((rows, D), BF),
                pltpu.VMEM((rows, D), BF),
                pltpu.VMEM((rows, units), BF),
                pltpu.VMEM((rows, units), BF),
                pltpu.VMEM((rows, units), BF),
                pltpu.VMEM((D, 2 * units), BF),
                pltpu.SemaphoreType.DMA((5 + units // D,)),
                pltpu.SemaphoreType.DMA((2, count)),
            ],
        ),
        out_shape=[
            jax.ShapeDtypeStruct((rows, D), BF),
            jax.ShapeDtypeStruct((sends, 2 * units), BF),
            jax.ShapeDtypeStruct((sends, 2 * units), BF),
        ],
        compiler_params=params(1, 36),
        cost_estimate=pl.CostEstimate(
            flops=8 * rows * D * units,
            bytes_accessed=rows * D * 6 + rows * units * 4 + D * units * 8,
            transcendentals=0,
        ),
        name="feed_back",
    )(place, weights, grad, normed, hidden, slope)


def attention_back_kernel(
    images,
    count,
    place,
    w_hbm,
    g_hbm,
    qk_hbm,
    v_hbm,
    r_hbm,
    pt_hbm,
    ff_hbm,
    normed_hbm,
    mixed_hbm,
    gain_ref,
    inverse_ref,
    ln_inverse_ref,
    sums_ref,
    out_ref,
    mine_ref,
    sent_ref,
    w_ref,
    g_ref,
    qk_ref,
    v_ref,
    r_ref,
    pt_ref,
    ff_ref,
    normed_ref,
    mixed_ref,
    d_qk_ref,
    d_qkv_ref,
    stage_ref,
    total_ref,
    gains_ref,
    low_ref,
    sems,
    mixed_sem,
    out_sems,
):
    section = place[0]
    pad = g_ref.shape[0] // images
    here = pl.ds(pl.multiple_of(section * HALF, HALF), HALF)

    def pairs_of(image):
        rows = pl.ds(pl.multiple_of(image * pad, pad), pad)
        pairs = [(pt_hbm.at[image], pt_ref.at[image])]
        for source, target in (
            (g_hbm, g_ref),
            (v_hbm, v_ref),
            (qk_hbm, qk_ref),
            (r_hbm, r_ref),
            (ff_hbm, ff_ref),
            (normed_hbm, normed_ref),
        ):
            pairs.append((source.at[rows, :], target.at[rows, :]))
        return pairs

    once = [(w_hbm.at[:, pl.ds(0, SPLIT)], w_ref), (mixed_hbm, mixed_ref)]
    copy_all(once[:1], mixed_sem, False)
    for image in range(images):
        copy_all(pairs_of(image), sems.at[image], False)
    pltpu.make_async_copy(once[1][0], once[1][1], mixed_sem.at[1]).start()
    total_ref[...] = jnp.zeros_like(total_ref)
    copy_all(once[:1], mixed_sem, True)

    def image_step(image, carry):
        rows = pl.ds(pl.multiple_of(image * pad, pad), pad)
        copy_all(pairs_of(image), sems.at[image], True)
        d_mixed = dot_nt(g_ref[rows, :], w_ref[here, :D]).astype(BF)
        attend_back(
            lambda pair: qk_ref[rows, pair * 128 : (pair + 1) * 128],
            lambda pair: qk_ref[rows, HALF + pair * 128 : HALF + (pair + 1) * 128],
            lambda pair: v_ref[rows, pair * 128 : (pair + 1) * 128],
            lambda head: pt_ref[image, head],
            d_mixed,
            d_qk_ref,
            d_qkv_ref,
            rows,
        )
        d_heads = d_qk_ref[...]
        shaped = qk_ref[rows, :].astype(F32) * inverse_ref[...]
        total_ref[1:2, :] += jnp.sum(d_heads * shaped, axis=0, keepdims=True)
        d_qkv_ref[rows, :D] = head_norm_back(d_heads, shaped, r_ref[rows, :].astype(F32), gain_ref[...])
        d_normed = dot_nt(d_qkv_ref[rows, :], w_ref[:, D:]) + ff_ref[rows, :].astype(F32)
        out_ref[rows, :] = d_normed.astype(BF)
        total_ref[0:1, :] += jnp.sum(d_normed * normed_ref[rows, :].astype(F32), axis=0, keepdims=True)
        return carry

    lax.fori_loop(0, images, image_step, 0)
    pltpu.make_async_copy(once[1][0], once[1][1], mixed_sem.at[1]).wait()
    gains_ref[...] = jnp.zeros_like(gains_ref)
    for block, source in enumerate((total_ref, sums_ref)):
        at = 3 * block
        gains_ref[at : at + 1, :D] = source[0:1, :] * ln_inverse_ref[block : block + 1, :]
        gains_ref[at + 1 : at + 2, here] = source[1:2, :HALF]
        gains_ref[at + 2 : at + 3, here] = source[1:2, HALF:]
    low_ref[...] = gains_ref[...].astype(BF)
    sends = D // 2
    made = []
    for which, target in enumerate((sent_ref, mine_ref)):
        made.append(
            pltpu.make_async_copy(low_ref, target.at[pl.ds(sends, 16), :], out_sems.at[count + which])
        )
    attention_grads(section, g_ref, normed_ref, mixed_ref, d_qkv_ref, stage_ref)
    made += spread(place, count, stage_ref, pl.ds(0, SPLIT), mine_ref, sent_ref, out_sems)
    for copy in made:
        copy.start()
    for copy in made:
        copy.wait()


def attention_back(tokens, place, count, grad, weights, qk_gain, ln_inverse, sums, normed, qk, v, r, pt, mixed, ff):
    rows = normed.shape[0]
    pad = pad_of(tokens)
    images = rows // pad
    sends = D // 2
    full = lambda shape: pl.BlockSpec(shape, lambda i, s: (0, 0))
    return pl.pallas_call(
        partial(attention_back_kernel, images, count),
        grid_spec=pltpu.PrefetchScalarGridSpec(
            num_scalar_prefetch=1,
            grid=(1,),
            in_specs=[ANYWHERE] * 9 + [full((1, D)), full((1, D)), full((2, D)), full((8, D))],
            out_specs=[full((rows, D)), ANYWHERE, ANYWHERE],
            scratch_shapes=[
                pltpu.VMEM((D, SPLIT), BF),
                pltpu.VMEM((rows, D), BF),
                pltpu.VMEM((rows, D), BF),
                pltpu.VMEM((rows, HALF), BF),
                pltpu.VMEM((rows, D), BF),
                pltpu.VMEM((images, 2 * PAIRS, pad, pad), BF),
                pltpu.VMEM((rows, D), BF),
                pltpu.VMEM((rows, D), BF),
                pltpu.VMEM((rows, HALF), BF),
                pltpu.VMEM((pad, D), F32),
                pltpu.VMEM((rows, 3 * HALF), BF),
                pltpu.VMEM((D, SPLIT), BF),
                pltpu.VMEM((8, D), F32),
                pltpu.VMEM((16, SPLIT), F32),
                pltpu.VMEM((16, SPLIT), BF),
                pltpu.SemaphoreType.DMA((images, 7)),
                pltpu.SemaphoreType.DMA((2,)),
                pltpu.SemaphoreType.DMA((count + 2,)),
            ],
        ),
        out_shape=[
            jax.ShapeDtypeStruct((rows, D), BF),
            jax.ShapeDtypeStruct((sends + 16, SPLIT), BF),
            jax.ShapeDtypeStruct((sends + 16, SPLIT), BF),
        ],
        compiler_params=params(1, 36),
        cost_estimate=pl.CostEstimate(
            flops=4 * rows * D * 4 * HALF + 16 * images * 6 * pad * pad * 64,
            bytes_accessed=rows * D * 16 + D * SPLIT * 4,
            transcendentals=0,
        ),
        name="attention_back",
    )(place, weights, grad, qk, v, r, pt, ff, normed, mixed, qk_gain, 1.0 / qk_gain, ln_inverse, sums)


def pack_kernel(count, place, qkv_ref, up_ref, proj_ref, down_ref, mine_ref, theirs_ref):
    rows = qkv_ref.shape[0]
    group = up_ref.shape[1] // (4 * count)
    section = place[0]
    up = up_ref[...].astype(F32)
    ups = []
    for part in range(4):
        pieces = [up[:, (4 * at + part) * group : (4 * at + part + 1) * group] for at in range(count)]
        ups.append(jnp.concatenate(pieces, axis=1).astype(BF))
    for half, target in ((section, mine_ref), (1 - section, theirs_ref)):
        target[:, :D] = proj_ref[...]
        for pair in range(3):
            source = pl.ds(pl.multiple_of(pair * D + half * HALF, HALF), HALF)
            target[:, D + pair * HALF : D + (pair + 1) * HALF] = qkv_ref[:, source]
        for part in range(2):
            at = SPLIT + part * D
            target[:, at : at + D] = jnp.where(half == 0, ups[part], ups[2 + part])
            at = SPLIT + (2 + part) * D
            source = pl.ds(pl.multiple_of((2 * half + part) * rows, rows), rows)
            target[:, at : at + D] = down_ref[source, :]


def pack(place, count, w_qkv, w_up, w_proj, w_down):
    rows = w_qkv.shape[0]
    width = SPLIT + w_up.shape[1]
    full = lambda value: pl.BlockSpec(value.shape, lambda i, s: (0, 0))
    shape = jax.ShapeDtypeStruct((rows, width), BF)
    return pl.pallas_call(
        partial(pack_kernel, count),
        grid_spec=pltpu.PrefetchScalarGridSpec(
            num_scalar_prefetch=1,
            grid=(1,),
            in_specs=[full(value) for value in (w_qkv, w_up, w_proj, w_down)],
            out_specs=[full(shape)] * 2,
        ),
        out_shape=[shape] * 2,
        compiler_params=params(1),
        name="pack",
    )(place, w_qkv, w_up, w_proj, w_down)


def finish_feed_kernel(count, place, sum_ref, arrived_ref, second_ref, second_arrived_ref, up_ref, down_ref):
    rows = sum_ref.shape[0]
    units = sum_ref.shape[1] // 2
    group = units // (2 * count)
    first = place[0] == 0
    low = jnp.where(first, sum_ref[...], second_arrived_ref[:, SPLIT:]).astype(F32)
    high = jnp.where(first, arrived_ref[...], second_ref[:, SPLIT:]).astype(F32)
    sources = (low, low, high, high)
    pieces = []
    for at in range(count):
        for part, source in enumerate(sources):
            column = part % 2 * D + at * group
            pieces.append(source[:, column : column + group])
    up_ref[...] = jnp.concatenate(pieces, axis=1)
    for part, source in enumerate(sources):
        column = units + part % 2 * D
        down_ref[part * rows : (part + 1) * rows, :] = source[:, column : column + D]


def finish_attention_kernel(
    place, sum_ref, arrived_ref, second_ref, second_arrived_ref, qkv_ref, proj_ref, ln_ref, query_ref, key_ref
):
    rows = qkv_ref.shape[0]
    first = place[0] == 0
    low = jnp.where(first, sum_ref[:rows, :], second_arrived_ref[:, :SPLIT]).astype(F32)
    high = jnp.where(first, arrived_ref[:rows, :], second_ref[:, :SPLIT]).astype(F32)
    proj_ref[...] = low[:, :D] + high[:, :D]
    for pair in range(3):
        at = D + pair * HALF
        qkv_ref[:, pair * D : pair * D + HALF] = low[:, at : at + HALF]
        qkv_ref[:, pair * D + HALF : (pair + 1) * D] = high[:, at : at + HALF]
    gains = sum_ref[rows:, :D].astype(F32) + arrived_ref[rows:, :D].astype(F32)
    for at, target in enumerate((ln_ref, query_ref, key_ref)):
        target[...] = jnp.where(first, gains[at : at + 1, :], gains[3 + at : 4 + at, :])


def finish(kernel, name, place, values, shapes):
    full = lambda value: pl.BlockSpec(value.shape, lambda i, s: (0, 0))
    shapes = [jax.ShapeDtypeStruct(shape, F32) for shape in shapes]
    return pl.pallas_call(
        kernel,
        grid_spec=pltpu.PrefetchScalarGridSpec(
            num_scalar_prefetch=1,
            grid=(1,),
            in_specs=[full(value) for value in values],
            out_specs=[full(shape) for shape in shapes],
        ),
        out_shape=shapes,
        compiler_params=params(1),
        name=name,
    )(place, *values)


def norm_backward_kernel(g_ref, x_ref, mine_ref, theirs_ref, ln_ref, out_ref):
    x = x_ref[...].astype(F32)
    centred = x - jnp.mean(x, axis=-1, keepdims=True)
    rstd = lax.rsqrt(jnp.mean(centred * centred, axis=-1, keepdims=True) + EPSILON)
    shaped = centred * rstd
    scaled = (mine_ref[...].astype(F32) + theirs_ref[...].astype(F32)) * ln_ref[...]
    d_x = rstd * (
        scaled
        - jnp.mean(scaled, axis=-1, keepdims=True)
        - shaped * jnp.mean(scaled * shaped, axis=-1, keepdims=True)
    )
    out_ref[...] = (g_ref[...].astype(F32) + d_x).astype(BF)


def norm_backward(grad, x, mine, theirs, ln_gain):
    rows = x.shape[0]
    block = pl.BlockSpec((rows // 4, D), lambda i: (i, 0))
    return pl.pallas_call(
        norm_backward_kernel,
        grid=(4,),
        in_specs=[block] * 4 + [pl.BlockSpec((1, D), lambda i: (0, 0))],
        out_specs=block,
        out_shape=jax.ShapeDtypeStruct((rows, D), BF),
        compiler_params=params(1),
        cost_estimate=pl.CostEstimate(flops=12 * rows * D, bytes_accessed=rows * D * 10, transcendentals=0),
        name="norm_backward",
    )(grad, x, mine, theirs, ln_gain)


def pad_of(tokens):
    return -(-tokens // 16) * 16


def relative(value, step):
    count = lax.axis_size("dp")
    return lax.ppermute(value, "dp", [(source, source ^ step) for source in range(count)])


def after(value, *others):
    return lax.optimization_barrier((value,) + others)[0]


def add_low(left, right):
    return (left.astype(F32) + right.astype(F32)).astype(BF)


def add_all(terms):
    result = terms[0].astype(F32)
    for term in terms[1:]:
        result = result + term.astype(F32)
    return result


def spread_rows(terms, count, place):
    at = jnp.arange(count // 2)
    device = (place[3] ^ (at % (count // 4))) * 4 + (place[2] ^ (at // (count // 4))) * 2
    shaped = terms.reshape(count, terms.shape[0] // count, terms.shape[1])
    return [shaped[device + core].reshape(-1, terms.shape[1]) for core in (place[1], 1 - place[1])]


def on_device(images, cotangent, w_qkv, w_up, w_proj, w_down, ln_gain, q_gain, k_gain):
    count = lax.axis_size("dp")
    section = lax.axis_index("section")
    first = section == 0
    me = lax.axis_index("dp")
    number, tokens, _ = images.shape
    pad = pad_of(tokens)
    rows = w_qkv.shape[1]
    group = w_down.shape[1] // 4
    units = w_up.shape[2] // 2

    def swap(value):
        return lax.ppermute(value, "section", [(0, 1), (1, 0)])

    def give(value, source):
        return lax.ppermute(value, "section", [(source, 1 - source)])

    place = jnp.stack([section, me % 2, (me // 2) % 2, me // 4]).astype(jnp.int32)
    aligned = rows % 16 == 0

    def attention_half(half):
        parts = [w_proj[0]]
        for pair in range(3):
            at = pair * D + half * HALF
            parts.append(w_qkv[0, :, at : at + HALF])
        return jnp.concatenate(parts, axis=1)

    def feed_half(half):
        ups = w_up[0].reshape(rows, count, 4, group)
        parts = []
        for part in (2 * half, 2 * half + 1):
            parts.append(ups[:, :, part].reshape(rows, count * group))
        for part in (2 * half, 2 * half + 1):
            parts.append(w_down[0, part * group : (part + 1) * group])
        return jnp.concatenate(parts, axis=1)

    if aligned:
        mine, theirs = pack(place, count, w_qkv[0], w_up[0], w_proj[0], w_down[0])
    else:
        low, high = (jnp.concatenate([attention_half(half), feed_half(half)], axis=1) for half in range(2))
        mine, theirs = jnp.where(first, low, high), jnp.where(first, high, low)
    other = swap(theirs)
    own_gains = jnp.concatenate([ln_gain, q_gain, k_gain], axis=0)
    their_gains = swap(own_gains)
    gains = (jnp.where(first, own_gains, their_gains), jnp.where(first, their_gains, own_gains))
    shards = (jnp.where(first, mine, after(other, their_gains)), jnp.where(first, other, mine))

    at_half = lambda gain: lax.dynamic_slice_in_dim(gain, section * HALF, HALF, 0)
    ln_gains = [gains[block][:1] for block in range(2)]
    qk_gains = [
        jnp.concatenate([at_half(gains[block][1]), at_half(gains[block][2])])[None] for block in range(2)
    ]

    def padded(value):
        return jnp.pad(value, ((0, 0), (0, pad - tokens), (0, 0))).reshape(number * pad, D)

    def trimmed(value):
        return value.reshape(number, pad, D)[:, :tokens]

    weights = []
    for block in range(2):
        shard = shards[block]
        if block == 1:
            shard = after(shard, weights[0][0])
        weights.append([lax.all_gather(shard, "dp", axis=0, tiled=True)])

    first_in = padded(images)
    none = jnp.stack([section, 0 * section]).astype(jnp.int32)
    saved = attention_forward(tokens, none, first_in, weights[0], ln_gains[0], qk_gains[0])
    hidden, slope, part = feed_forward(none, units, saved[0], weights[0], saved[6])
    kept = tuple(saved[:6]) + (hidden, slope)
    middle = (first_in.astype(F32) + part.astype(F32) + swap(part).astype(F32)).astype(BF)

    grad = padded(cotangent)
    halves, last_parts, parts, theirs, sums_1 = [], [], [], [], 0
    for half in range(2):
        last_half, part, sums, normed, mixed, hidden, d_up, d_qkv = whole_block(
            tokens, units, place, middle, grad, weights[1][0], ln_gains[1], qk_gains[1], half, 2
        )
        own = slice(half * (number // 2) * pad, (half + 1) * (number // 2) * pad)
        halves.append((hidden, grad[own], normed, d_up, mixed, d_qkv))
        last_parts.append(last_half)
        parts.append(part)
        theirs.append(swap(part))
        sums_1 = sums_1 + sums
    halves[1] = (after(halves[1][0], theirs[0]),) + halves[1][1:]
    terms = weight_grads(place, units, halves)
    second_sum = lax.psum_scatter(terms, "dp", scatter_dimension=0, tiled=True)
    middle_grad = norm_backward(
        after(grad, terms), middle, jnp.concatenate(parts), jnp.concatenate(theirs), ln_gains[1]
    )
    last_part = jnp.concatenate(last_parts)

    quarter = count // 4 * rows
    if aligned:
        feed_part, mine, sent = feed_back(place, units, count, middle_grad, weights[0][0], kept[0], *kept[6:])
    else:
        terms, feed_part = feed_backward(none, units, middle_grad, kept[0], weights[0], *kept[6:])
        mine, sent = spread_rows(terms, count, place)
    total = add_low(mine, relative(sent, 1))
    sent = total[quarter:]
    arrived = relative(sent, 2)
    ln_inverse = 1.0 / jnp.concatenate(ln_gains, axis=0)
    attention_in = after(middle_grad, sent)
    if aligned:
        part, mine, sent = attention_back(
            tokens, place, count, attention_in, weights[0][0], qk_gains[0], ln_inverse, sums_1, *kept[:6], feed_part
        )
    else:
        terms, part, sums_0 = attention_backward(
            tokens, none, attention_in, weights[0], qk_gains[0], *kept[:6], feed_part
        )
        mine, sent = spread_rows(terms, count, place)
        gain_rows = jnp.zeros((16, SPLIT), F32)
        for block, sums in enumerate((sums_0, sums_1)):
            gain_rows = gain_rows.at[3 * block, :D].set(sums[0] * ln_inverse[block])
            for kind in range(2):
                value = sums[1:2, kind * HALF : (kind + 1) * HALF]
                gain_rows = lax.dynamic_update_slice(gain_rows, value, (3 * block + 1 + kind, section * HALF))
        mine, sent = (jnp.concatenate([value, gain_rows.astype(BF)], axis=0) for value in (mine, sent))
    far_total = add_low(total[:quarter], arrived)
    far = range(1, count // 4)
    feed_terms = [far_total[:rows]]
    for step in far:
        feed_terms.append(relative(far_total[step * rows : (step + 1) * rows], 4 * step))

    total = add_low(mine, relative(after(sent, far_total), 1))
    sent = total[quarter:]
    arrived = relative(sent, 2)
    theirs = give(part, 1)
    last_theirs = give(after(last_part, part), 0)
    far_total = add_low(total[:quarter], arrived[:quarter])
    gain_total = add_low(total[2 * quarter :], arrived[quarter:])
    attention_terms = [jnp.concatenate([far_total[:rows], gain_total], axis=0)]
    for step in far:
        message = jnp.concatenate([far_total[step * rows : (step + 1) * rows], gain_total], axis=0)
        attention_terms.append(relative(message, 4 * step))
    second_theirs = give(second_sum, 0)
    feed_sum = add_all([after(feed_terms[0], far_total)] + feed_terms[1:]).astype(BF)
    feed_theirs = give(feed_sum, 1)
    attention_sum = add_all([after(attention_terms[0], feed_sum, second_theirs, theirs)] + attention_terms[1:]).astype(BF)
    attention_theirs = swap(attention_sum)

    first_grad = norm_backward(middle_grad, first_in, after(part, attention_sum), theirs, ln_gains[0])
    input_grads = trimmed(jnp.where(first, first_grad, middle_grad))
    last_theirs = after(last_theirs, feed_sum)
    last = middle.astype(F32) + last_part.astype(F32) + last_theirs.astype(F32)
    outputs = trimmed(jnp.where(first, middle, last.astype(BF)))

    if aligned:
        grad_up, grad_down = finish(
            partial(finish_feed_kernel, count),
            "finish_feed",
            place,
            (feed_sum, feed_theirs, second_sum, second_theirs),
            ((rows, 2 * units), (4 * rows, D)),
        )
        grad_qkv, grad_proj, grad_ln, grad_q, grad_k = finish(
            finish_attention_kernel,
            "finish_attention",
            place,
            (attention_sum, attention_theirs, second_sum, second_theirs),
            ((rows, 3 * D), (rows, D), (1, D), (1, D), (1, D)),
        )
        return (
            outputs[None],
            input_grads[None],
            grad_qkv[None],
            grad_up[None],
            grad_proj[None],
            grad_down[None],
            grad_ln,
            grad_q,
            grad_k,
        )

    def halves_of(own, theirs):
        own, theirs = own.astype(F32), theirs.astype(F32)
        return jnp.where(first, own, theirs), jnp.where(first, theirs, own)

    own = jnp.where(first, feed_sum, second_sum[:, SPLIT:])
    other = jnp.where(first, feed_theirs, second_theirs[:, SPLIT:])
    ups, downs = [], []
    for source in halves_of(own, other):
        for part in range(2):
            at = part * D
            ups.append(source[:, at : at + D].reshape(rows, count, 1, group))
            downs.append(source[:, units + at : units + at + D])
    grad_up = jnp.concatenate(ups, axis=2).reshape(rows, 2 * units)
    grad_down = jnp.concatenate(downs, axis=0)

    own = jnp.where(first, attention_sum[:rows], second_sum[:, :SPLIT])
    other = jnp.where(first, attention_theirs[:rows], second_theirs[:, :SPLIT])
    low_half, high_half = halves_of(own, other)
    grad_proj = low_half[:, :D] + high_half[:, :D]
    pieces = []
    for pair in range(3):
        at = slice(D + pair * HALF, D + (pair + 1) * HALF)
        pieces += [low_half[:, at], high_half[:, at]]
    grad_qkv = jnp.concatenate(pieces, axis=1)
    totals = attention_sum[rows : rows + 6, :D].astype(F32) + attention_theirs[rows : rows + 6, :D].astype(F32)
    totals = jnp.where(first, totals[:3], totals[3:])
    return (
        outputs[None],
        input_grads[None],
        grad_qkv[None],
        grad_up[None],
        grad_proj[None],
        grad_down[None],
        totals[0:1],
        totals[1:2],
        totals[2:3],
    )


def solution(mesh):
    placed = (
        P("dp", None, None),
        P("dp", None, None),
        P("section", "dp", None),
        P("section", "dp", None),
        P("section", "dp", None),
        P("section", "dp", None),
        P("section", None),
        P("section", None),
        P("section", None),
    )
    return jax.shard_map(
        on_device,
        mesh=mesh,
        in_specs=placed,
        out_specs=(
            P("section", "dp", None, None),
            P("section", "dp", None, None),
            P("section", "dp", None),
            P("section", "dp", None),
            P("section", "dp", None),
            P("section", "dp", None),
            P("section", None),
            P("section", None),
            P("section", None),
        ),
        check_vma=False,
    )
```

```python
from functools import partial

import jax
import jax.numpy as jnp
from jax import lax
from jax.experimental import pallas as pl
from jax.experimental.pallas import tpu as pltpu
from jax.sharding import PartitionSpec as P

D = 768
HEADS = 12
HEAD = 64
HALF = D // 2
PAIRS = HALF // 128
EPSILON = 1e-06
TILE = 256
BF = jnp.bfloat16
F32 = jnp.float32
SPLIT = D + 3 * HALF
ANYWHERE = pl.BlockSpec(memory_space=pltpu.HBM)
C0 = 0.7978845608028654
C1 = 0.044715


def dot(a, b):
    return lax.dot_general(a, b, (((1,), (0,)), ((), ())), preferred_element_type=F32)


def dot_nt(a, b):
    return lax.dot_general(a, b, (((1,), (1,)), ((), ())), preferred_element_type=F32)


def dot_tn(a, b):
    return lax.dot_general(a, b, (((0,), (0,)), ((), ())), preferred_element_type=F32)


def head_means(x):
    row = lax.broadcasted_iota(jnp.int32, (256, 256), 0) // HEAD
    col = lax.broadcasted_iota(jnp.int32, (256, 256), 1) // HEAD
    ones = jnp.where(row == col, 1.0 / HEAD, 0.0).astype(BF)
    high = x.astype(BF)
    rest = (x - high.astype(F32)).astype(BF)
    parts = []
    for at in range(0, x.shape[1], 256):
        parts.append(dot(high[:, at : at + 256], ones) + dot(rest[:, at : at + 256], ones))
    return jnp.concatenate(parts, axis=1)


def half_mask(rows, h):
    return lax.broadcasted_iota(jnp.int32, (rows, 128), 1) // HEAD == h


def params(steps, megabytes=20):
    return pltpu.CompilerParams(
        dimension_semantics=("arbitrary",) * steps, vmem_limit_bytes=megabytes * 1024 * 1024
    )


def copies(place, pieces, columns, dest_ref, sems):
    made = []
    for step, piece in enumerate(pieces):
        rows = piece.shape[0]
        at = pl.ds(pl.multiple_of((place[1] ^ step) * rows, rows), rows)
        made.append(pltpu.make_async_copy(piece.at[:, columns], dest_ref.at[at, :], sems.at[step]))
    return made


def attention_forward_kernel(tokens, count, place, *refs):
    pieces = refs[:count]
    (
        x_ref,
        ln_ref,
        gain_ref,
        normed_ref,
        qk_ref,
        v_ref,
        r_ref,
        pt_ref,
        mixed_ref,
        part_ref,
        w_ref,
        sems,
    ) = refs[count:]
    section = place[0]

    @pl.when(pl.program_id(0) == 0)
    def _():
        for copy in copies(place, pieces, slice(0, SPLIT), w_ref, sems):
            copy.start()

    x = x_ref[...].astype(F32)
    rows = x.shape[0]
    pad = rows // 2
    centred = x - jnp.mean(x, axis=-1, keepdims=True)
    spread = jnp.mean(centred * centred, axis=-1, keepdims=True)
    normed = (centred * lax.rsqrt(spread + EPSILON) * ln_ref[...]).astype(BF)
    normed_ref[...] = normed

    @pl.when(pl.program_id(0) == 0)
    def _():
        for copy in copies(place, pieces, slice(0, SPLIT), w_ref, sems):
            copy.wait()

    qkv = dot(normed, w_ref[:, D:])
    qk = qkv[:, :D]
    centred = qk - head_means(qk)
    rstd = lax.rsqrt(head_means(centred * centred) + EPSILON)
    qk_ref[...] = (centred * rstd * gain_ref[...]).astype(BF)
    r_ref[...] = rstd.astype(BF)
    v_ref[...] = qkv[:, D:].astype(BF)
    valid = lax.broadcasted_iota(jnp.int32, (pad, pad), 0) < tokens
    for image in range(2):
        at = slice(image * pad, (image + 1) * pad)
        for pair in range(PAIRS):
            query = qk_ref[at, pair * 128 : (pair + 1) * 128]
            key = qk_ref[at, HALF + pair * 128 : HALF + (pair + 1) * 128]
            value = v_ref[at, pair * 128 : (pair + 1) * 128]
            mixed = jnp.zeros((pad, 128), F32)
            for h in range(2):
                mask = half_mask(pad, h)
                scores = dot_nt(jnp.where(mask, key, 0), query) * HEAD ** (-0.5)
                scores = jnp.where(valid, scores, -1e30)
                top = jnp.max(scores, axis=0, keepdims=True)
                weights = jnp.exp(scores - top)
                probs = weights * (1.0 / jnp.sum(weights, axis=0, keepdims=True))
                probs = probs.astype(BF)
                pt_ref[image, 2 * pair + h] = probs
                mixed += dot_tn(probs, jnp.where(mask, value, 0))
            mixed_ref[at, pair * 128 : (pair + 1) * 128] = mixed.astype(BF)
    proj = w_ref[pl.ds(pl.multiple_of(section * HALF, HALF), HALF), :D]
    part_ref[...] = dot(mixed_ref[...], proj).astype(BF)


def attention_forward(tokens, place, x, pieces, ln_gain, qk_gain):
    rows = x.shape[0]
    images = rows // pad_of(tokens)
    pad = pad_of(tokens)
    step = 2 * pad
    row = lambda width: pl.BlockSpec((step, width), lambda i, s: (i, 0))
    full = lambda shape: pl.BlockSpec(shape, lambda i, s: (0, 0), pipeline_mode=pl.Buffered(1))
    return pl.pallas_call(
        partial(attention_forward_kernel, tokens, len(pieces)),
        grid_spec=pltpu.PrefetchScalarGridSpec(
            num_scalar_prefetch=1,
            grid=(images // 2,),
            in_specs=[ANYWHERE] * len(pieces) + [row(D), full((1, D)), full((1, D))],
            out_specs=[
                row(D),
                row(D),
                row(HALF),
                row(D),
                pl.BlockSpec((2, 2 * PAIRS, pad, pad), lambda i, s: (i, 0, 0, 0)),
                row(HALF),
                row(D),
            ],
            scratch_shapes=[
                pltpu.VMEM((D, SPLIT), BF),
                pltpu.SemaphoreType.DMA((len(pieces),)),
            ],
        ),
        out_shape=[
            jax.ShapeDtypeStruct((rows, D), BF),
            jax.ShapeDtypeStruct((rows, D), BF),
            jax.ShapeDtypeStruct((rows, HALF), BF),
            jax.ShapeDtypeStruct((rows, D), BF),
            jax.ShapeDtypeStruct((images, 2 * PAIRS, pad, pad), BF),
            jax.ShapeDtypeStruct((rows, HALF), BF),
            jax.ShapeDtypeStruct((rows, D), BF),
        ],
        compiler_params=params(1),
        cost_estimate=pl.CostEstimate(
            flops=2 * rows * D * (3 * HALF + HALF) + 8 * images * 6 * pad * pad * 64,
            bytes_accessed=rows * D * 12 + D * 1920 * 2,
            transcendentals=images * 6 * pad * pad,
        ),
        name="attention_forward",
    )(place, *pieces, x, ln_gain, qk_gain)


def feed_copies(place, pieces, units, up_ref, down_ref, sems):
    base = pieces[0].shape[1] - 2 * units
    ups = copies(place, pieces, slice(base, base + units), up_ref, sems.at[0])
    downs = []
    for part in range(units // D):
        columns = slice(base + units + part * D, base + units + (part + 1) * D)
        downs += copies(place, pieces, columns, down_ref.at[part], sems.at[1 + part])
    return ups, downs


def feed_tiles(step):
    across = D // TILE
    columns = pl.ds(pl.multiple_of(step * TILE, TILE), TILE)
    return columns, step // across, pl.ds(pl.multiple_of((step % across) * TILE, TILE), TILE)


def feed_forward_kernel(steps, count, place, *refs):
    pieces = refs[:count]
    normed_ref, part_ref, hidden_ref, slope_ref, out_ref, acc_ref, up_ref, down_ref, sems = refs[count:]
    step = pl.program_id(0)
    columns, part, rows = feed_tiles(step)

    @pl.when(step == 0)
    def _():
        ups, downs = feed_copies(place, pieces, steps * TILE, up_ref, down_ref, sems)
        for copy in ups + downs:
            copy.start()
        for copy in ups + downs:
            copy.wait()

    up = dot(normed_ref[...], up_ref[:, columns])
    square = up * up
    tanh = jnp.tanh(C0 * up * (1.0 + C1 * square))
    hidden = (0.5 * up * (1.0 + tanh)).astype(BF)
    slope = 0.5 * (1.0 + tanh) + (0.5 * C0) * up * (1.0 - tanh * tanh) * (1.0 + (3.0 * C1) * square)
    hidden_ref[...] = hidden
    slope_ref[...] = slope.astype(BF)
    term = dot(hidden, down_ref[part, rows, :])

    @pl.when(step == 0)
    def _():
        acc_ref[...] = part_ref[...].astype(F32) + term

    @pl.when(step > 0)
    def _():
        acc_ref[...] += term

    @pl.when(step == steps - 1)
    def _():
        out_ref[...] = acc_ref[...].astype(BF)


def feed_scratch(rows, units, count):
    return [
        pltpu.VMEM((rows, D), F32),
        pltpu.VMEM((D, units), BF),
        pltpu.VMEM((units // D, D, D), BF),
        pltpu.SemaphoreType.DMA((1 + units // D, count)),
    ]


def feed_forward(place, units, normed, pieces, part):
    rows = normed.shape[0]
    steps = units // TILE
    whole = pl.BlockSpec((rows, D), lambda j, s: (0, 0))
    tile = pl.BlockSpec((rows, TILE), lambda j, s: (0, j))
    return pl.pallas_call(
        partial(feed_forward_kernel, steps, len(pieces)),
        grid_spec=pltpu.PrefetchScalarGridSpec(
            num_scalar_prefetch=1,
            grid=(steps,),
            in_specs=[ANYWHERE] * len(pieces) + [whole, whole],
            out_specs=[tile, tile, whole],
            scratch_shapes=feed_scratch(rows, units, len(pieces)),
        ),
        out_shape=[
            jax.ShapeDtypeStruct((rows, units), BF),
            jax.ShapeDtypeStruct((rows, units), BF),
            jax.ShapeDtypeStruct((rows, D), BF),
        ],
        compiler_params=params(1),
        cost_estimate=pl.CostEstimate(
            flops=4 * rows * D * units,
            bytes_accessed=rows * D * 6 + rows * units * 4 + D * units * 4,
            transcendentals=rows * units,
        ),
        name="feed_forward",
    )(place, *pieces, normed, part)


def feed_backward_kernel(steps, count, place, *refs):
    pieces = refs[:count]
    g_ref, normed_ref, hidden_ref, slope_ref, grad_ref, out_ref, acc_ref, up_ref, down_ref, sems = refs[count:]
    step = pl.program_id(0)
    columns, part, rows = feed_tiles(step)

    @pl.when(step == 0)
    def _():
        ups, downs = feed_copies(place, pieces, steps * TILE, up_ref, down_ref, sems)
        for copy in downs + ups:
            copy.start()
        for copy in downs + ups:
            copy.wait()

    grad = g_ref[...]
    d_up = (slope_ref[...].astype(F32) * dot_nt(grad, down_ref[part, rows, :])).astype(BF)
    there = pl.ds(pl.multiple_of(steps * TILE + part * D, D), D)
    grad_ref[rows, there] = dot_tn(hidden_ref[...], grad).astype(BF)
    grad_ref[:, columns] = dot_tn(normed_ref[...], d_up).astype(BF)
    term = dot_nt(d_up, up_ref[:, columns])

    @pl.when(step == 0)
    def _():
        acc_ref[...] = term

    @pl.when(step > 0)
    def _():
        acc_ref[...] += term

    @pl.when(step == steps - 1)
    def _():
        out_ref[...] = acc_ref[...].astype(BF)


def feed_backward(place, units, grad, normed, pieces, hidden, slope):
    rows = normed.shape[0]
    steps = units // TILE
    whole = pl.BlockSpec((rows, D), lambda j, s: (0, 0))
    tile = pl.BlockSpec((rows, TILE), lambda j, s: (0, j))
    return pl.pallas_call(
        partial(feed_backward_kernel, steps, len(pieces)),
        grid_spec=pltpu.PrefetchScalarGridSpec(
            num_scalar_prefetch=1,
            grid=(steps,),
            in_specs=[ANYWHERE] * len(pieces) + [whole, whole, tile, tile],
            out_specs=[pl.BlockSpec((D, 2 * units), lambda j, s: (0, 0)), whole],
            scratch_shapes=feed_scratch(rows, units, len(pieces)),
        ),
        out_shape=[
            jax.ShapeDtypeStruct((D, 2 * units), BF),
            jax.ShapeDtypeStruct((rows, D), BF),
        ],
        compiler_params=params(1),
        cost_estimate=pl.CostEstimate(
            flops=8 * rows * D * units,
            bytes_accessed=rows * D * 6 + rows * units * 4 + D * units * 8,
            transcendentals=0,
        ),
        name="feed_backward",
    )(place, *pieces, grad, normed, hidden, slope)


def attention_backward_kernel(steps, count, place, *refs):
    pieces = refs[:count]
    (
        g_ref,
        gain_ref,
        inverse_ref,
        normed_ref,
        qk_ref,
        v_ref,
        r_ref,
        pt_ref,
        mixed_ref,
        ff_ref,
        grad_ref,
        out_ref,
        sums_ref,
        qkv_acc,
        proj_acc,
        d_qk,
        d_qkv,
        w_ref,
        sems,
    ) = refs[count:]
    step = pl.program_id(0)
    section = place[0]
    rows = g_ref.shape[0]
    pad = rows // 2

    @pl.when(step == 0)
    def _():
        for copy in copies(place, pieces, slice(0, SPLIT), w_ref, sems):
            copy.start()
        sums_ref[...] = jnp.zeros_like(sums_ref)
        for copy in copies(place, pieces, slice(0, SPLIT), w_ref, sems):
            copy.wait()

    grad = g_ref[...]
    here = pl.ds(pl.multiple_of(section * HALF, HALF), HALF)
    d_mixed = dot_nt(grad, w_ref[here, :D]).astype(BF)
    proj_term = dot_tn(mixed_ref[...], grad)
    for image in range(2):
        at = slice(image * pad, (image + 1) * pad)
        for pair in range(PAIRS):
            lanes = slice(pair * 128, (pair + 1) * 128)
            key_lanes = slice(HALF + pair * 128, HALF + (pair + 1) * 128)
            query = qk_ref[at, lanes]
            key = qk_ref[at, key_lanes]
            value = v_ref[at, lanes]
            d_mix = d_mixed[at, lanes]
            d_query = jnp.zeros((pad, 128), F32)
            d_key = jnp.zeros((pad, 128), F32)
            d_value = jnp.zeros((pad, 128), F32)
            for h in range(2):
                mask = half_mask(pad, h)
                d_mix_head = jnp.where(mask, d_mix, 0)
                probs_low = pt_ref[image, 2 * pair + h]
                probs = probs_low.astype(F32)
                d_probs = dot_nt(value, d_mix_head)
                weighted = jnp.sum(probs * d_probs, axis=0, keepdims=True)
                d_scores = (probs * (d_probs - weighted)).astype(BF)
                d_value += dot(probs_low, d_mix_head)
                d_key += dot(d_scores, jnp.where(mask, query, 0))
                d_query += dot_tn(d_scores, jnp.where(mask, key, 0))
            d_qk[at, lanes] = d_query * HEAD ** (-0.5)
            d_qk[at, key_lanes] = d_key * HEAD ** (-0.5)
            d_qkv[at, D + pair * 128 : D + (pair + 1) * 128] = d_value.astype(BF)
    d_normed_heads = d_qk[...]
    shaped = qk_ref[...].astype(F32) * inverse_ref[...]
    sums_ref[1:2, :] += jnp.sum(d_normed_heads * shaped, axis=0, keepdims=True)
    scaled = d_normed_heads * gain_ref[...]
    d_qkv[:, :D] = (
        r_ref[...].astype(F32) * (scaled - head_means(scaled) - shaped * head_means(scaled * shaped))
    ).astype(BF)
    normed = normed_ref[...]
    qkv_term = dot_tn(normed, d_qkv[...])
    d_normed = dot_nt(d_qkv[...], w_ref[:, D:]) + ff_ref[...].astype(F32)
    out_ref[...] = d_normed.astype(BF)
    sums_ref[0:1, :] += jnp.sum(d_normed * normed.astype(F32), axis=0, keepdims=True)

    @pl.when(step == 0)
    def _():
        qkv_acc[...] = qkv_term
        proj_acc[...] = proj_term

    @pl.when(step > 0)
    def _():
        qkv_acc[...] += qkv_term
        proj_acc[...] += proj_term

    @pl.when(step == steps - 1)
    def _():
        there = pl.ds(pl.multiple_of((1 - section) * HALF, HALF), HALF)
        grad_ref[here, :D] = proj_acc[...].astype(BF)
        grad_ref[there, :D] = jnp.zeros((HALF, D), BF)
        grad_ref[:, D:] = qkv_acc[...].astype(BF)


def attention_backward(tokens, place, grad, pieces, qk_gain, normed, qk, v, r, pt, mixed, ff):
    rows = normed.shape[0]
    pad = pad_of(tokens)
    images = rows // pad
    step = 2 * pad
    steps = images // 2
    width = SPLIT
    row = lambda columns: pl.BlockSpec((step, columns), lambda i, s: (i, 0))
    full = lambda shape: pl.BlockSpec(shape, lambda i, s: (0, 0), pipeline_mode=pl.Buffered(1))
    return pl.pallas_call(
        partial(attention_backward_kernel, steps, len(pieces)),
        grid_spec=pltpu.PrefetchScalarGridSpec(
            num_scalar_prefetch=1,
            grid=(steps,),
            in_specs=[ANYWHERE] * len(pieces)
            + [
                row(D),
                full((1, D)),
                full((1, D)),
                row(D),
                row(D),
                row(HALF),
                row(D),
                pl.BlockSpec((2, 2 * PAIRS, pad, pad), lambda i, s: (i, 0, 0, 0)),
                row(HALF),
                row(D),
            ],
            out_specs=[
                pl.BlockSpec((D, width), lambda i, s: (0, 0)),
                row(D),
                pl.BlockSpec((8, D), lambda i, s: (0, 0)),
            ],
            scratch_shapes=[
                pltpu.VMEM((D, 3 * HALF), F32),
                pltpu.VMEM((HALF, D), F32),
                pltpu.VMEM((step, D), F32),
                pltpu.VMEM((step, 3 * HALF), BF),
                pltpu.VMEM((D, SPLIT), BF),
                pltpu.SemaphoreType.DMA((len(pieces),)),
            ],
        ),
        out_shape=[
            jax.ShapeDtypeStruct((D, width), BF),
            jax.ShapeDtypeStruct((rows, D), BF),
            jax.ShapeDtypeStruct((8, D), F32),
        ],
        compiler_params=params(1),
        cost_estimate=pl.CostEstimate(
            flops=4 * rows * D * 4 * HALF + 16 * images * 6 * pad * pad * 64,
            bytes_accessed=rows * D * 16 + D * width * 4,
            transcendentals=0,
        ),
        name="attention_backward",
    )(place, *pieces, grad, qk_gain, 1.0 / qk_gain, normed, qk, v, r, pt, mixed, ff)


def copy_all(pairs, sems, wait):
    for at, (source, target) in enumerate(pairs):
        copy = pltpu.make_async_copy(source, target, sems.at[at])
        if wait:
            copy.wait()
        else:
            copy.start()


def weight_pairs(w_ref, units, attention_ref, up_ref, down_ref):
    pairs = [
        (w_ref.at[:, pl.ds(0, SPLIT)], attention_ref),
        (w_ref.at[:, pl.ds(SPLIT, units)], up_ref),
    ]
    for part in range(units // D):
        pairs.append((w_ref.at[:, pl.ds(SPLIT + units + part * D, D)], down_ref.at[part]))
    return pairs


def gelu(up):
    square = up * up
    tanh = jnp.tanh(up * (C0 + (C0 * C1) * square))
    share = 0.5 + 0.5 * tanh
    slope = share + up * (share * (1.0 - share)) * (2.0 * C0 + (6.0 * C0 * C1) * square)
    return (up * share).astype(BF), slope


def attend(tokens, qk_ref, v_ref, pt_ref, mixed_ref, rows):
    pad = v_ref.shape[0]
    valid = lax.broadcasted_iota(jnp.int32, (pad, pad), 0) < tokens
    for pair in range(PAIRS):
        lanes = slice(pair * 128, (pair + 1) * 128)
        query = qk_ref[:, lanes]
        key = qk_ref[:, HALF + pair * 128 : HALF + (pair + 1) * 128]
        value = v_ref[:, lanes]
        mixed = jnp.zeros((pad, 128), F32)
        for h in range(2):
            mask = half_mask(pad, h)
            scores = dot_nt(jnp.where(mask, key, 0), query) * HEAD ** (-0.5)
            scores = jnp.where(valid, scores, -1e30)
            top = jnp.max(scores, axis=0, keepdims=True)
            powers = jnp.exp(scores - top)
            probs = (powers * (1.0 / jnp.sum(powers, axis=0, keepdims=True))).astype(BF)
            pt_ref[2 * pair + h] = probs
            mixed += dot_tn(probs, jnp.where(mask, value, 0))
        mixed_ref[rows, lanes] = mixed.astype(BF)


def attend_back(query_of, key_of, value_of, probs_of, d_mixed, d_qk_ref, d_qkv_ref, rows):
    pad = d_mixed.shape[0]
    for pair in range(PAIRS):
        lanes = slice(pair * 128, (pair + 1) * 128)
        query, key, value = query_of(pair), key_of(pair), value_of(pair)
        d_mix = d_mixed[:, lanes]
        d_query = jnp.zeros((pad, 128), F32)
        d_key = jnp.zeros((pad, 128), F32)
        d_value = jnp.zeros((pad, 128), F32)
        for h in range(2):
            mask = half_mask(pad, h)
            d_mix_head = jnp.where(mask, d_mix, 0)
            probs_low = probs_of(2 * pair + h)
            probs = probs_low.astype(F32)
            d_probs = dot_nt(value, d_mix_head)
            weighted = jnp.sum(probs * d_probs, axis=0, keepdims=True)
            d_scores = (probs * (d_probs - weighted)).astype(BF)
            d_value += dot(probs_low, d_mix_head)
            d_key += dot(d_scores, jnp.where(mask, query, 0))
            d_query += dot_tn(d_scores, jnp.where(mask, key, 0))
        d_qk_ref[:, lanes] = d_query * HEAD ** (-0.5)
        d_qk_ref[:, HALF + pair * 128 : HALF + (pair + 1) * 128] = d_key * HEAD ** (-0.5)
        d_qkv_ref[rows, D + pair * 128 : D + (pair + 1) * 128] = d_value.astype(BF)


def head_norm_back(d_heads, shaped, rstd, gain):
    scaled = d_heads * gain
    return (rstd * (scaled - head_means(scaled) - shaped * head_means(scaled * shaped))).astype(BF)


def whole_block_kernel(
    tokens,
    images,
    units,
    place,
    w_ref,
    x_ref,
    g_ref,
    ln_ref,
    gain_ref,
    part_ref,
    out_ref,
    sums_ref,
    normed_hbm,
    mixed_hbm,
    hidden_hbm,
    d_up_hbm,
    d_qkv_hbm,
    attention_ref,
    up_ref,
    down_ref,
    normed_ref,
    mixed_ref,
    hidden_ref,
    d_up_ref,
    d_qkv_ref,
    qk_ref,
    v_ref,
    shaped_ref,
    rstd_ref,
    pt_ref,
    slope_ref,
    d_qk_ref,
    sems,
    out_sems,
):
    section = place[0]
    pairs = weight_pairs(w_ref, units, attention_ref, up_ref, down_ref)
    copy_all(pairs, sems, False)
    sums_ref[...] = jnp.zeros_like(sums_ref)
    pad = x_ref.shape[0] // images
    here = pl.ds(pl.multiple_of(section * HALF, HALF), HALF)

    def leaving(image):
        rows = pl.ds(pl.multiple_of(image * pad, pad), pad)
        made = []
        for source, target in (
            (normed_ref, normed_hbm),
            (mixed_ref, mixed_hbm),
            (hidden_ref, hidden_hbm),
            (d_up_ref, d_up_hbm),
            (d_qkv_ref, d_qkv_hbm),
        ):
            made.append((source.at[rows, :], target.at[rows, :]))
        return made

    copy_all(pairs, sems, True)

    def image_step(image, carry):
        rows = pl.ds(pl.multiple_of(image * pad, pad), pad)
        x = x_ref[rows, :].astype(F32)
        centred = x - jnp.mean(x, axis=-1, keepdims=True)
        spread = jnp.mean(centred * centred, axis=-1, keepdims=True)
        normed = (centred * lax.rsqrt(spread + EPSILON) * ln_ref[...]).astype(BF)
        normed_ref[rows, :] = normed
        qkv = dot(normed, attention_ref[:, D:])
        qk = qkv[:, :D]
        centred = qk - head_means(qk)
        rstd = lax.rsqrt(head_means(centred * centred) + EPSILON)
        rstd_ref[...] = rstd
        shaped = centred * rstd
        shaped_ref[...] = shaped
        qk_ref[...] = (shaped * gain_ref[...]).astype(BF)
        v_ref[...] = qkv[:, D:].astype(BF)
        attend(tokens, qk_ref, v_ref, pt_ref, mixed_ref, rows)
        part = dot(mixed_ref[rows, :], attention_ref[here, :D])
        grad = g_ref[rows, :]
        hidden, slope = gelu(dot(normed, up_ref[...]))
        hidden_ref[rows, :] = hidden
        slope_ref[...] = slope
        for at in range(units // D):
            columns = slice(at * D, (at + 1) * D)
            part += dot(hidden[:, columns], down_ref[at])
            d_up_ref[rows, columns] = (slope_ref[:, columns] * dot_nt(grad, down_ref[at])).astype(BF)
        part_ref[rows, :] = part.astype(BF)
        d_normed = dot_nt(d_up_ref[rows, :], up_ref[...])
        d_mixed = dot_nt(grad, attention_ref[here, :D]).astype(BF)
        attend_back(
            lambda pair: qk_ref[:, pair * 128 : (pair + 1) * 128],
            lambda pair: qk_ref[:, HALF + pair * 128 : HALF + (pair + 1) * 128],
            lambda pair: v_ref[:, pair * 128 : (pair + 1) * 128],
            lambda head: pt_ref[head],
            d_mixed,
            d_qk_ref,
            d_qkv_ref,
            rows,
        )
        d_heads = d_qk_ref[...]
        shaped = shaped_ref[...]
        sums_ref[1:2, :] += jnp.sum(d_heads * shaped, axis=0, keepdims=True)
        d_qkv_ref[rows, :D] = head_norm_back(d_heads, shaped, rstd_ref[...], gain_ref[...])
        d_normed += dot_nt(d_qkv_ref[rows, :], attention_ref[:, D:])
        out_ref[rows, :] = d_normed.astype(BF)
        sums_ref[0:1, :] += jnp.sum(d_normed * normed_ref[rows, :].astype(F32), axis=0, keepdims=True)
        copy_all(leaving(image), out_sems.at[image], False)
        return carry

    lax.fori_loop(0, images, image_step, 0)
    for image in range(images):
        copy_all(leaving(image), out_sems.at[image], True)


def weight_grads_kernel(units, halves, count, place, *refs):
    sources = [refs[6 * half : 6 * half + 6] for half in range(halves)]
    refs = refs[6 * halves :]
    outs = (refs[:2], refs[2:4]) if count else (refs[:1], refs[1:2])
    hidden_ref, g_ref, normed_ref, d_up_ref, mixed_ref, d_qkv_ref, feed_ref, attention_ref, sems, out_sems = refs[-10:]
    targets = (hidden_ref, g_ref, normed_ref, d_up_ref, mixed_ref, d_qkv_ref)
    pairs = []
    for half in range(halves):
        rows = sources[half][0].shape[0]
        at = pl.ds(half * rows, rows)
        pairs.append([(source, target.at[at, :]) for source, target in zip(sources[half], targets)])
    for half in range(halves):
        copy_all(pairs[half], sems.at[half], False)
    for half in range(halves):
        copy_all(pairs[half], sems.at[half], True)
    section = place[0]
    made = []
    for at, stage in enumerate((feed_ref, attention_ref)):
        if at == 0:
            feed_grads(units, g_ref, normed_ref, hidden_ref, d_up_ref, stage, 0)
        else:
            attention_grads(section, g_ref, normed_ref, mixed_ref, d_qkv_ref, stage)
        if count:
            new = spread(place, count, stage, pl.ds(0, stage.shape[1]), *outs[at], out_sems.at[at])
        else:
            new = [pltpu.make_async_copy(stage, outs[at][0], out_sems.at[at, 0])]
        for copy in new:
            copy.start()
        made += new
    for copy in made:
        copy.wait()


def weight_grads(place, units, halves, count):
    rows = sum(half[0].shape[0] for half in halves)
    shapes = []
    for width in (2 * units, SPLIT):
        shapes += [jax.ShapeDtypeStruct((D // 2, width), BF)] * 2 if count else [jax.ShapeDtypeStruct((D, width), BF)]
    return pl.pallas_call(
        partial(weight_grads_kernel, units, len(halves), count),
        grid_spec=pltpu.PrefetchScalarGridSpec(
            num_scalar_prefetch=1,
            grid=(1,),
            in_specs=[ANYWHERE] * (6 * len(halves)),
            out_specs=[ANYWHERE] * len(shapes),
            scratch_shapes=[
                pltpu.VMEM((rows, units), BF),
                pltpu.VMEM((rows, D), BF),
                pltpu.VMEM((rows, D), BF),
                pltpu.VMEM((rows, units), BF),
                pltpu.VMEM((rows, HALF), BF),
                pltpu.VMEM((rows, 3 * HALF), BF),
                pltpu.VMEM((D, 2 * units), BF),
                pltpu.VMEM((D, SPLIT), BF),
                pltpu.SemaphoreType.DMA((len(halves), 6)),
                pltpu.SemaphoreType.DMA((2, max(count, 1))),
            ],
        ),
        out_shape=shapes,
        compiler_params=params(1, 30),
        cost_estimate=pl.CostEstimate(
            flops=2 * rows * D * (4 * HALF + 2 * units),
            bytes_accessed=rows * (2 * units + 6 * HALF + 2 * D) * 2 + D * (SPLIT + 2 * units) * 2,
            transcendentals=0,
        ),
        name="weight_grads",
    )(place, *[value for half in halves for value in half])


def copy_all_from(pairs, first, sems):
    for at in range(first, len(pairs)):
        pltpu.make_async_copy(pairs[at][0], pairs[at][1], sems.at[at]).wait()


def feed_grads(units, g_ref, normed_ref, hidden_ref, d_up_ref, stage_ref, base):
    for at in range(0, units, 512):
        stage_ref[:, base + at : base + at + 512] = dot_tn(normed_ref[...], d_up_ref[:, at : at + 512]).astype(BF)
    for at in range(0, units, 384):
        rows = slice(at % D, at % D + 384)
        columns = slice(base + units + at // D * D, base + units + at // D * D + D)
        stage_ref[rows, columns] = dot_tn(hidden_ref[:, at : at + 384], g_ref[...]).astype(BF)


def attention_grads(section, g_ref, normed_ref, mixed_ref, d_qkv_ref, stage_ref):
    here = pl.ds(pl.multiple_of(section * HALF, HALF), HALF)
    there = pl.ds(pl.multiple_of((1 - section) * HALF, HALF), HALF)
    stage_ref[here, :D] = dot_tn(mixed_ref[...], g_ref[...]).astype(BF)
    stage_ref[there, :D] = jnp.zeros((HALF, D), BF)
    for at in range(0, 3 * HALF, 384):
        stage_ref[:, D + at : D + at + 384] = dot_tn(normed_ref[...], d_qkv_ref[:, at : at + 384]).astype(BF)


def whole_block(tokens, units, place, x, grad, weights, ln_gain, qk_gain, half, halves):
    rows = x.shape[0]
    pad = pad_of(tokens)
    images = rows // pad
    full = lambda shape: pl.BlockSpec(shape, lambda i, s: (0, 0))
    own = pl.BlockSpec((rows, D), lambda i, s: (half, 0))
    widths = (D, HALF, units, units, 3 * HALF)
    return pl.pallas_call(
        partial(whole_block_kernel, tokens, images, units),
        grid_spec=pltpu.PrefetchScalarGridSpec(
            num_scalar_prefetch=1,
            grid=(1,),
            in_specs=[ANYWHERE, full((rows, D)), own, full((1, D)), full((1, D))],
            out_specs=[full((rows, D)), full((rows, D)), full((8, D))] + [ANYWHERE] * 5,
            scratch_shapes=[
                pltpu.VMEM((D, SPLIT), BF),
                pltpu.VMEM((D, units), BF),
                pltpu.VMEM((units // D, D, D), BF),
            ]
            + [pltpu.VMEM((rows, width), BF) for width in widths]
            + [
                pltpu.VMEM((pad, D), BF),
                pltpu.VMEM((pad, HALF), BF),
                pltpu.VMEM((pad, D), F32),
                pltpu.VMEM((pad, D), F32),
                pltpu.VMEM((2 * PAIRS, pad, pad), BF),
                pltpu.VMEM((pad, units), F32),
                pltpu.VMEM((pad, D), F32),
                pltpu.SemaphoreType.DMA((2 + units // D,)),
                pltpu.SemaphoreType.DMA((images, 5)),
            ],
        ),
        out_shape=[
            jax.ShapeDtypeStruct((rows, D), BF),
            jax.ShapeDtypeStruct((rows, D), BF),
            jax.ShapeDtypeStruct((8, D), F32),
        ]
        + [jax.ShapeDtypeStruct((rows, width), BF) for width in widths],
        compiler_params=params(1, 28),
        cost_estimate=pl.CostEstimate(
            flops=4 * rows * D * (4 * HALF + 2 * units),
            bytes_accessed=rows * D * 20 + D * (SPLIT + 2 * units) * 2,
            transcendentals=rows * units,
        ),
        name="whole_block",
    )(place, weights, x, grad, ln_gain, qk_gain)


def spread(place, count, stage_ref, columns, mine_ref, sent_ref, sems):
    core, near, far = place[1], place[2], place[3]
    rows = stage_ref.shape[0] // count
    made = []
    for which, target in enumerate((sent_ref, mine_ref)):
        for at in range(count // 2):
            other, step = at // (count // 4), at % (count // 4)
            device = (far ^ step) * 4 + (near ^ other) * 2 + (core if which else 1 - core)
            source = stage_ref.at[pl.ds(pl.multiple_of(device * rows, rows), rows), columns]
            made.append(
                pltpu.make_async_copy(
                    source, target.at[pl.ds(at * rows, rows), columns], sems.at[which * (count // 2) + at]
                )
            )
    return made


def feed_back_kernel(
    images,
    units,
    count,
    place,
    w_ref,
    g_hbm,
    normed_hbm,
    hidden_hbm,
    slope_hbm,
    out_ref,
    mine_ref,
    sent_ref,
    up_ref,
    down_ref,
    g_ref,
    normed_ref,
    hidden_ref,
    slope_ref,
    d_up_ref,
    stage_ref,
    sems,
    out_sems,
):
    pairs = []
    for part in range(units // D):
        pairs.append((w_ref.at[:, pl.ds(SPLIT + units + part * D, D)], down_ref.at[part]))
    pairs += [
        (g_hbm, g_ref),
        (slope_hbm, slope_ref),
        (w_ref.at[:, pl.ds(SPLIT, units)], up_ref),
        (hidden_hbm, hidden_ref),
        (normed_hbm, normed_ref),
    ]
    ready = len(pairs) - 2
    copy_all(pairs, sems, False)
    copy_all(pairs[:ready], sems, True)
    pad = g_ref.shape[0] // images

    def image_step(image, carry):
        rows = pl.ds(pl.multiple_of(image * pad, pad), pad)
        grad = g_ref[rows, :]
        for at in range(units // D):
            columns = slice(at * D, (at + 1) * D)
            d_up_ref[rows, columns] = (
                slope_ref[rows, columns].astype(F32) * dot_nt(grad, down_ref[at])
            ).astype(BF)
        out_ref[rows, :] = dot_nt(d_up_ref[rows, :], up_ref[...]).astype(BF)
        return carry

    lax.fori_loop(0, images, image_step, 0)
    copy_all_from(pairs, ready, sems)
    for at in range(0, units, 384):
        rows = slice(at % D, at % D + 384)
        columns = slice(units + at // D * D, units + at // D * D + D)
        stage_ref[rows, columns] = dot_tn(hidden_ref[:, at : at + 384], g_ref[...]).astype(BF)
    downs = spread(place, count, stage_ref, pl.ds(units, units), mine_ref, sent_ref, out_sems.at[0])
    for copy in downs:
        copy.start()
    for at in range(0, units, 512):
        stage_ref[:, at : at + 512] = dot_tn(normed_ref[...], d_up_ref[:, at : at + 512]).astype(BF)
    ups = spread(place, count, stage_ref, pl.ds(0, units), mine_ref, sent_ref, out_sems.at[1])
    for copy in ups:
        copy.start()
    for copy in downs + ups:
        copy.wait()


def feed_back(place, units, count, grad, weights, normed, hidden, slope):
    rows = normed.shape[0]
    images = 4 if rows % 64 == 0 else 1
    sends = D // 2
    return pl.pallas_call(
        partial(feed_back_kernel, images, units, count),
        grid_spec=pltpu.PrefetchScalarGridSpec(
            num_scalar_prefetch=1,
            grid=(1,),
            in_specs=[ANYWHERE] * 5,
            out_specs=[pl.BlockSpec((rows, D), lambda i, s: (0, 0)), ANYWHERE, ANYWHERE],
            scratch_shapes=[
                pltpu.VMEM((D, units), BF),
                pltpu.VMEM((units // D, D, D), BF),
                pltpu.VMEM((rows, D), BF),
                pltpu.VMEM((rows, D), BF),
                pltpu.VMEM((rows, units), BF),
                pltpu.VMEM((rows, units), BF),
                pltpu.VMEM((rows, units), BF),
                pltpu.VMEM((D, 2 * units), BF),
                pltpu.SemaphoreType.DMA((5 + units // D,)),
                pltpu.SemaphoreType.DMA((2, count)),
            ],
        ),
        out_shape=[
            jax.ShapeDtypeStruct((rows, D), BF),
            jax.ShapeDtypeStruct((sends, 2 * units), BF),
            jax.ShapeDtypeStruct((sends, 2 * units), BF),
        ],
        compiler_params=params(1, 58),
        cost_estimate=pl.CostEstimate(
            flops=8 * rows * D * units,
            bytes_accessed=rows * D * 6 + rows * units * 4 + D * units * 8,
            transcendentals=0,
        ),
        name="feed_back",
    )(place, weights, grad, normed, hidden, slope)


def attention_back_kernel(
    images,
    count,
    place,
    w_hbm,
    g_hbm,
    qk_hbm,
    v_hbm,
    r_hbm,
    pt_hbm,
    ff_hbm,
    normed_hbm,
    mixed_hbm,
    gain_ref,
    inverse_ref,
    ln_inverse_ref,
    sums_ref,
    out_ref,
    mine_ref,
    sent_ref,
    w_ref,
    g_ref,
    qk_ref,
    v_ref,
    r_ref,
    pt_ref,
    ff_ref,
    normed_ref,
    mixed_ref,
    d_qk_ref,
    d_qkv_ref,
    stage_ref,
    total_ref,
    gains_ref,
    low_ref,
    sems,
    mixed_sem,
    out_sems,
):
    section = place[0]
    pad = g_ref.shape[0] // images
    here = pl.ds(pl.multiple_of(section * HALF, HALF), HALF)

    def pairs_of(image):
        rows = pl.ds(pl.multiple_of(image * pad, pad), pad)
        pairs = [(pt_hbm.at[image], pt_ref.at[image])]
        for source, target in (
            (g_hbm, g_ref),
            (v_hbm, v_ref),
            (qk_hbm, qk_ref),
            (r_hbm, r_ref),
            (ff_hbm, ff_ref),
            (normed_hbm, normed_ref),
        ):
            pairs.append((source.at[rows, :], target.at[rows, :]))
        return pairs

    once = [(w_hbm.at[:, pl.ds(0, SPLIT)], w_ref), (mixed_hbm, mixed_ref)]
    copy_all(once[:1], mixed_sem, False)
    for image in range(images):
        copy_all(pairs_of(image), sems.at[image], False)
    pltpu.make_async_copy(once[1][0], once[1][1], mixed_sem.at[1]).start()
    total_ref[...] = jnp.zeros_like(total_ref)
    copy_all(once[:1], mixed_sem, True)

    def image_step(image, carry):
        rows = pl.ds(pl.multiple_of(image * pad, pad), pad)
        copy_all(pairs_of(image), sems.at[image], True)
        d_mixed = dot_nt(g_ref[rows, :], w_ref[here, :D]).astype(BF)
        attend_back(
            lambda pair: qk_ref[rows, pair * 128 : (pair + 1) * 128],
            lambda pair: qk_ref[rows, HALF + pair * 128 : HALF + (pair + 1) * 128],
            lambda pair: v_ref[rows, pair * 128 : (pair + 1) * 128],
            lambda head: pt_ref[image, head],
            d_mixed,
            d_qk_ref,
            d_qkv_ref,
            rows,
        )
        d_heads = d_qk_ref[...]
        shaped = qk_ref[rows, :].astype(F32) * inverse_ref[...]
        total_ref[1:2, :] += jnp.sum(d_heads * shaped, axis=0, keepdims=True)
        d_qkv_ref[rows, :D] = head_norm_back(d_heads, shaped, r_ref[rows, :].astype(F32), gain_ref[...])
        d_normed = dot_nt(d_qkv_ref[rows, :], w_ref[:, D:]) + ff_ref[rows, :].astype(F32)
        out_ref[rows, :] = d_normed.astype(BF)
        total_ref[0:1, :] += jnp.sum(d_normed * normed_ref[rows, :].astype(F32), axis=0, keepdims=True)
        return carry

    lax.fori_loop(0, images, image_step, 0)
    pltpu.make_async_copy(once[1][0], once[1][1], mixed_sem.at[1]).wait()
    gains_ref[...] = jnp.zeros_like(gains_ref)
    for block, source in enumerate((total_ref, sums_ref)):
        at = 3 * block
        gains_ref[at : at + 1, :D] = source[0:1, :] * ln_inverse_ref[block : block + 1, :]
        gains_ref[at + 1 : at + 2, here] = source[1:2, :HALF]
        gains_ref[at + 2 : at + 3, here] = source[1:2, HALF:]
    low_ref[...] = gains_ref[...].astype(BF)
    sends = D // 2
    made = []
    for which, target in enumerate((sent_ref, mine_ref)):
        made.append(
            pltpu.make_async_copy(low_ref, target.at[pl.ds(sends, 16), :], out_sems.at[count + which])
        )
    attention_grads(section, g_ref, normed_ref, mixed_ref, d_qkv_ref, stage_ref)
    made += spread(place, count, stage_ref, pl.ds(0, SPLIT), mine_ref, sent_ref, out_sems)
    for copy in made:
        copy.start()
    for copy in made:
        copy.wait()


def attention_back(tokens, place, count, grad, weights, qk_gain, ln_inverse, sums, normed, qk, v, r, pt, mixed, ff):
    rows = normed.shape[0]
    pad = pad_of(tokens)
    images = rows // pad
    sends = D // 2
    full = lambda shape: pl.BlockSpec(shape, lambda i, s: (0, 0))
    return pl.pallas_call(
        partial(attention_back_kernel, images, count),
        grid_spec=pltpu.PrefetchScalarGridSpec(
            num_scalar_prefetch=1,
            grid=(1,),
            in_specs=[ANYWHERE] * 9 + [full((1, D)), full((1, D)), full((2, D)), full((8, D))],
            out_specs=[full((rows, D)), ANYWHERE, ANYWHERE],
            scratch_shapes=[
                pltpu.VMEM((D, SPLIT), BF),
                pltpu.VMEM((rows, D), BF),
                pltpu.VMEM((rows, D), BF),
                pltpu.VMEM((rows, HALF), BF),
                pltpu.VMEM((rows, D), BF),
                pltpu.VMEM((images, 2 * PAIRS, pad, pad), BF),
                pltpu.VMEM((rows, D), BF),
                pltpu.VMEM((rows, D), BF),
                pltpu.VMEM((rows, HALF), BF),
                pltpu.VMEM((pad, D), F32),
                pltpu.VMEM((rows, 3 * HALF), BF),
                pltpu.VMEM((D, SPLIT), BF),
                pltpu.VMEM((8, D), F32),
                pltpu.VMEM((16, SPLIT), F32),
                pltpu.VMEM((16, SPLIT), BF),
                pltpu.SemaphoreType.DMA((images, 7)),
                pltpu.SemaphoreType.DMA((2,)),
                pltpu.SemaphoreType.DMA((count + 2,)),
            ],
        ),
        out_shape=[
            jax.ShapeDtypeStruct((rows, D), BF),
            jax.ShapeDtypeStruct((sends + 16, SPLIT), BF),
            jax.ShapeDtypeStruct((sends + 16, SPLIT), BF),
        ],
        compiler_params=params(1, 58),
        cost_estimate=pl.CostEstimate(
            flops=4 * rows * D * 4 * HALF + 16 * images * 6 * pad * pad * 64,
            bytes_accessed=rows * D * 16 + D * SPLIT * 4,
            transcendentals=0,
        ),
        name="attention_back",
    )(place, weights, grad, qk, v, r, pt, ff, normed, mixed, qk_gain, 1.0 / qk_gain, ln_inverse, sums)


def pack_kernel(count, place, qkv_ref, up_ref, proj_ref, down_ref, mine_ref, theirs_ref):
    rows = qkv_ref.shape[0]
    group = up_ref.shape[1] // (4 * count)
    section = place[0]
    up = up_ref[...].astype(F32)
    ups = []
    for part in range(4):
        pieces = [up[:, (4 * at + part) * group : (4 * at + part + 1) * group] for at in range(count)]
        ups.append(jnp.concatenate(pieces, axis=1).astype(BF))
    for half, target in ((section, mine_ref), (1 - section, theirs_ref)):
        target[:, :D] = proj_ref[...]
        for pair in range(3):
            source = pl.ds(pl.multiple_of(pair * D + half * HALF, HALF), HALF)
            target[:, D + pair * HALF : D + (pair + 1) * HALF] = qkv_ref[:, source]
        for part in range(2):
            at = SPLIT + part * D
            target[:, at : at + D] = jnp.where(half == 0, ups[part], ups[2 + part])
            at = SPLIT + (2 + part) * D
            source = pl.ds(pl.multiple_of((2 * half + part) * rows, rows), rows)
            target[:, at : at + D] = down_ref[source, :]


def pack(place, count, w_qkv, w_up, w_proj, w_down):
    rows = w_qkv.shape[0]
    width = SPLIT + w_up.shape[1]
    full = lambda value: pl.BlockSpec(value.shape, lambda i, s: (0, 0))
    shape = jax.ShapeDtypeStruct((rows, width), BF)
    return pl.pallas_call(
        partial(pack_kernel, count),
        grid_spec=pltpu.PrefetchScalarGridSpec(
            num_scalar_prefetch=1,
            grid=(1,),
            in_specs=[full(value) for value in (w_qkv, w_up, w_proj, w_down)],
            out_specs=[full(shape)] * 2,
        ),
        out_shape=[shape] * 2,
        compiler_params=params(1),
        name="pack",
    )(place, w_qkv, w_up, w_proj, w_down)


def finish_feed_kernel(count, place, sum_ref, arrived_ref, second_ref, second_arrived_ref, up_ref, down_ref):
    rows = sum_ref.shape[0]
    units = sum_ref.shape[1] // 2
    group = units // (2 * count)
    first = place[0] == 0
    low = jnp.where(first, sum_ref[...], second_arrived_ref[...]).astype(F32)
    high = jnp.where(first, arrived_ref[...], second_ref[...]).astype(F32)
    sources = (low, low, high, high)
    pieces = []
    for at in range(count):
        for part, source in enumerate(sources):
            column = part % 2 * D + at * group
            pieces.append(source[:, column : column + group])
    up_ref[...] = jnp.concatenate(pieces, axis=1)
    for part, source in enumerate(sources):
        column = units + part % 2 * D
        down_ref[part * rows : (part + 1) * rows, :] = source[:, column : column + D]


def finish_attention_kernel(
    place, sum_ref, arrived_ref, second_ref, second_arrived_ref, qkv_ref, proj_ref, ln_ref, query_ref, key_ref
):
    rows = qkv_ref.shape[0]
    first = place[0] == 0
    low = jnp.where(first, sum_ref[:rows, :], second_arrived_ref[...]).astype(F32)
    high = jnp.where(first, arrived_ref[:rows, :], second_ref[...]).astype(F32)
    proj_ref[...] = low[:, :D] + high[:, :D]
    for pair in range(3):
        at = D + pair * HALF
        qkv_ref[:, pair * D : pair * D + HALF] = low[:, at : at + HALF]
        qkv_ref[:, pair * D + HALF : (pair + 1) * D] = high[:, at : at + HALF]
    gains = sum_ref[rows:, :D].astype(F32) + arrived_ref[rows:, :D].astype(F32)
    for at, target in enumerate((ln_ref, query_ref, key_ref)):
        target[...] = jnp.where(first, gains[at : at + 1, :], gains[3 + at : 4 + at, :])


def finish(kernel, name, place, values, shapes):
    full = lambda value: pl.BlockSpec(value.shape, lambda i, s: (0, 0))
    shapes = [jax.ShapeDtypeStruct(shape, F32) for shape in shapes]
    return pl.pallas_call(
        kernel,
        grid_spec=pltpu.PrefetchScalarGridSpec(
            num_scalar_prefetch=1,
            grid=(1,),
            in_specs=[full(value) for value in values],
            out_specs=[full(shape) for shape in shapes],
        ),
        out_shape=shapes,
        compiler_params=params(1),
        name=name,
    )(place, *values)


def assemble_kernel(count, place, *refs):
    out_ref, sems = refs[count:]
    made = copies(place, refs[:count], slice(None), out_ref, sems)
    for copy in made:
        copy.start()
    for copy in made:
        copy.wait()


def assemble(place, pieces):
    rows, width = pieces[0].shape
    return pl.pallas_call(
        partial(assemble_kernel, len(pieces)),
        grid_spec=pltpu.PrefetchScalarGridSpec(
            num_scalar_prefetch=1,
            grid=(1,),
            in_specs=[ANYWHERE] * len(pieces),
            out_specs=ANYWHERE,
            scratch_shapes=[pltpu.SemaphoreType.DMA((len(pieces),))],
        ),
        out_shape=jax.ShapeDtypeStruct((len(pieces) * rows, width), BF),
        compiler_params=params(1),
        name="assemble",
    )(place, *pieces)


def forward_block_kernel(tokens, images, units, count, half, chained, place, *refs):
    pieces, refs = refs[:count], refs[count:]
    x_ref, ln_ref, gain_ref = refs[:3]
    refs = refs[3 + (8 if chained else 0) :]
    part_ref, homes = refs[0], refs[1:9]
    attention_ref, up_ref, down_ref = refs[9:12]
    kept = refs[12:20]
    normed_ref, qk_ref, v_ref, r_ref, pt_ref, mixed_ref, hidden_ref, slope_ref = kept
    total_ref, attention_sems, feed_sems, out_sems = refs[20:]
    pad = x_ref.shape[0] // images
    here = pl.ds(pl.multiple_of(place[0] * HALF, HALF), HALF)
    attention_copies = copies(place, pieces, slice(0, SPLIT), attention_ref, attention_sems)
    feed_copies = copies(place, pieces, slice(SPLIT, SPLIT + units), up_ref, feed_sems.at[0])
    for part in range(units // D):
        columns = slice(SPLIT + units + part * D, SPLIT + units + (part + 1) * D)
        feed_copies += copies(place, pieces, columns, down_ref.at[part], feed_sems.at[1 + part])
    for copy in attention_copies + feed_copies:
        copy.start()

    def leaving(image, which):
        rows = pl.ds(pl.multiple_of(image * pad, pad), pad)
        there = pl.ds(pl.multiple_of((half * images + image) * pad, pad), pad)
        made = []
        for at in which:
            if at == 4:
                made.append((kept[at].at[image], homes[at].at[half * images + image]))
            else:
                made.append((kept[at].at[rows, :], homes[at].at[there, :]))
        return made

    for copy in attention_copies:
        copy.wait()

    def attention_step(image, carry):
        rows = pl.ds(pl.multiple_of(image * pad, pad), pad)
        x = x_ref[rows, :].astype(F32)
        centred = x - jnp.mean(x, axis=-1, keepdims=True)
        spread = jnp.mean(centred * centred, axis=-1, keepdims=True)
        normed = (centred * lax.rsqrt(spread + EPSILON) * ln_ref[...]).astype(BF)
        normed_ref[rows, :] = normed
        qkv = dot(normed, attention_ref[:, D:])
        qk = qkv[:, :D]
        centred = qk - head_means(qk)
        rstd = lax.rsqrt(head_means(centred * centred) + EPSILON)
        r_ref[rows, :] = rstd.astype(BF)
        qk_ref[rows, :] = (centred * rstd * gain_ref[...]).astype(BF)
        v_ref[rows, :] = qkv[:, D:].astype(BF)
        attend(tokens, qk_ref.at[rows, :], v_ref.at[rows, :], pt_ref.at[image], mixed_ref, rows)
        total_ref[rows, :] = dot(mixed_ref[rows, :], attention_ref[here, :D])
        copy_all(leaving(image, range(6)), out_sems.at[image, 0], False)
        return carry

    lax.fori_loop(0, images, attention_step, 0)
    for copy in feed_copies:
        copy.wait()

    def feed_step(image, carry):
        rows = pl.ds(pl.multiple_of(image * pad, pad), pad)
        hidden, slope = gelu(dot(normed_ref[rows, :], up_ref[...]))
        hidden_ref[rows, :] = hidden
        slope_ref[rows, :] = slope.astype(BF)
        part = total_ref[rows, :]
        for at in range(units // D):
            part += dot(hidden[:, at * D : (at + 1) * D], down_ref[at])
        part_ref[rows, :] = part.astype(BF)
        copy_all(leaving(image, (6, 7)), out_sems.at[image, 1], False)
        return carry

    lax.fori_loop(0, images, feed_step, 0)
    for image in range(images):
        copy_all(leaving(image, range(6)), out_sems.at[image, 0], True)
        copy_all(leaving(image, (6, 7)), out_sems.at[image, 1], True)


def forward_block(tokens, units, place, x, pieces, ln_gain, qk_gain, half, halves, kept):
    pad = pad_of(tokens)
    whole = x.shape[0]
    rows = whole // halves
    images = rows // pad
    count = len(pieces)
    full = lambda shape: pl.BlockSpec(shape, lambda i, s: (0, 0))
    widths = (D, D, HALF, D, None, HALF, units, units)

    def shape_of(width, size):
        return (size // pad, 2 * PAIRS, pad, pad) if width is None else (size, width)

    first = 1 + count + 3
    return pl.pallas_call(
        partial(forward_block_kernel, tokens, images, units, count, half, len(kept) > 0),
        grid_spec=pltpu.PrefetchScalarGridSpec(
            num_scalar_prefetch=1,
            grid=(1,),
            in_specs=[ANYWHERE] * count
            + [pl.BlockSpec((rows, D), lambda i, s: (half, 0)), full((1, D)), full((1, D))]
            + [ANYWHERE] * len(kept),
            out_specs=[full((rows, D))] + [ANYWHERE] * 8,
            scratch_shapes=[
                pltpu.VMEM((D, SPLIT), BF),
                pltpu.VMEM((D, units), BF),
                pltpu.VMEM((units // D, D, D), BF),
            ]
            + [pltpu.VMEM(shape_of(width, rows), BF) for width in widths]
            + [
                pltpu.VMEM((rows, D), F32),
                pltpu.SemaphoreType.DMA((count,)),
                pltpu.SemaphoreType.DMA((1 + units // D, count)),
                pltpu.SemaphoreType.DMA((images, 2, 6)),
            ],
        ),
        out_shape=[jax.ShapeDtypeStruct((rows, D), BF)]
        + [jax.ShapeDtypeStruct(shape_of(width, whole), BF) for width in widths],
        input_output_aliases={first + at: 1 + at for at in range(len(kept))},
        compiler_params=params(1, 58),
        cost_estimate=pl.CostEstimate(
            flops=2 * rows * D * (4 * HALF + 2 * units),
            bytes_accessed=rows * D * 20 + D * (SPLIT + 2 * units) * 2,
            transcendentals=rows * units,
        ),
        name="forward_block",
    )(place, *pieces, x, ln_gain, qk_gain, *kept)


def norm_backward_kernel(g_ref, x_ref, mine_ref, theirs_ref, ln_ref, out_ref):
    x = x_ref[...].astype(F32)
    centred = x - jnp.mean(x, axis=-1, keepdims=True)
    rstd = lax.rsqrt(jnp.mean(centred * centred, axis=-1, keepdims=True) + EPSILON)
    shaped = centred * rstd
    scaled = (mine_ref[...].astype(F32) + theirs_ref[...].astype(F32)) * ln_ref[...]
    d_x = rstd * (
        scaled
        - jnp.mean(scaled, axis=-1, keepdims=True)
        - shaped * jnp.mean(scaled * shaped, axis=-1, keepdims=True)
    )
    out_ref[...] = (g_ref[...].astype(F32) + d_x).astype(BF)


def norm_backward(grad, x, mine, theirs, ln_gain):
    rows = x.shape[0]
    block = pl.BlockSpec((rows // 4, D), lambda i: (i, 0))
    return pl.pallas_call(
        norm_backward_kernel,
        grid=(4,),
        in_specs=[block] * 4 + [pl.BlockSpec((1, D), lambda i: (0, 0))],
        out_specs=block,
        out_shape=jax.ShapeDtypeStruct((rows, D), BF),
        compiler_params=params(1),
        cost_estimate=pl.CostEstimate(flops=12 * rows * D, bytes_accessed=rows * D * 10, transcendentals=0),
        name="norm_backward",
    )(grad, x, mine, theirs, ln_gain)


def pad_of(tokens):
    return -(-tokens // 16) * 16


def relative(value, step):
    count = lax.axis_size("dp")
    return lax.ppermute(value, "dp", [(source, source ^ step) for source in range(count)])


def after(value, *others):
    return lax.optimization_barrier((value,) + others)[0]


def gather_far(shard):
    count = lax.axis_size("dp")
    return [shard] + [relative(shard, 4 * far) for far in range(1, count // 4)]


def gather_near(quads):
    nears = [relative(piece, 2) for piece in quads]
    pieces = []
    for left, right in zip(quads, nears):
        pieces += [left, relative(left, 1), right, relative(right, 1)]
    return pieces


def beside(values, other):
    return lax.optimization_barrier(tuple(values) + (other,))[:-1]


def add_low(left, right):
    return (left.astype(F32) + right.astype(F32)).astype(BF)


def add_all(terms):
    result = terms[0].astype(F32)
    for term in terms[1:]:
        result = result + term.astype(F32)
    return result


def spread_rows(terms, count, place):
    at = jnp.arange(count // 2)
    device = (place[3] ^ (at % (count // 4))) * 4 + (place[2] ^ (at // (count // 4))) * 2
    shaped = terms.reshape(count, terms.shape[0] // count, terms.shape[1])
    return [shaped[device + core].reshape(-1, terms.shape[1]) for core in (place[1], 1 - place[1])]


def on_device(images, cotangent, w_qkv, w_up, w_proj, w_down, ln_gain, q_gain, k_gain):
    count = lax.axis_size("dp")
    section = lax.axis_index("section")
    first = section == 0
    me = lax.axis_index("dp")
    number, tokens, _ = images.shape
    pad = pad_of(tokens)
    rows = w_qkv.shape[1]
    group = w_down.shape[1] // 4
    units = w_up.shape[2] // 2

    def swap(value):
        return lax.ppermute(value, "section", [(0, 1), (1, 0)])

    def give(value, source):
        return lax.ppermute(value, "section", [(source, 1 - source)])

    place = jnp.stack([section, me % 2, (me // 2) % 2, me // 4]).astype(jnp.int32)
    aligned = rows % 16 == 0

    def attention_half(half):
        parts = [w_proj[0]]
        for pair in range(3):
            at = pair * D + half * HALF
            parts.append(w_qkv[0, :, at : at + HALF])
        return jnp.concatenate(parts, axis=1)

    def feed_half(half):
        ups = w_up[0].reshape(rows, count, 4, group)
        parts = []
        for part in (2 * half, 2 * half + 1):
            parts.append(ups[:, :, part].reshape(rows, count * group))
        for part in (2 * half, 2 * half + 1):
            parts.append(w_down[0, part * group : (part + 1) * group])
        return jnp.concatenate(parts, axis=1)

    if aligned:
        mine, theirs = pack(place, count, w_qkv[0], w_up[0], w_proj[0], w_down[0])
    else:
        low, high = (jnp.concatenate([attention_half(half), feed_half(half)], axis=1) for half in range(2))
        mine, theirs = jnp.where(first, low, high), jnp.where(first, high, low)
    other = swap(theirs)
    own_gains = jnp.concatenate([ln_gain, q_gain, k_gain], axis=0)
    their_gains = swap(own_gains)
    gains = (jnp.where(first, own_gains, their_gains), jnp.where(first, their_gains, own_gains))
    shards = (jnp.where(first, mine, after(other, their_gains)), jnp.where(first, other, mine))

    at_half = lambda gain: lax.dynamic_slice_in_dim(gain, section * HALF, HALF, 0)
    ln_gains = [gains[block][:1] for block in range(2)]
    qk_gains = [
        jnp.concatenate([at_half(gains[block][1]), at_half(gains[block][2])])[None] for block in range(2)
    ]

    def padded(value):
        return jnp.pad(value, ((0, 0), (0, pad - tokens), (0, 0))).reshape(number * pad, D)

    def trimmed(value):
        return value.reshape(number, pad, D)[:, :tokens]

    if aligned:
        quads = gather_far(shards[0])
        pieces = gather_near(quads)
        started = quads + [pieces[6]]
        none = jnp.stack([section, me]).astype(jnp.int32)
    else:
        pieces = [lax.all_gather(shards[0], "dp", axis=0, tiled=True)]
        started = pieces
        none = jnp.stack([section, 0 * me]).astype(jnp.int32)
    second_weights = lax.all_gather(after(shards[1], *started), "dp", axis=0, tiled=True)

    first_in = padded(images)
    kept, swapped, middles = (), [], []
    for half in range(2):
        part, *kept = forward_block(
            tokens, units, none, first_in, pieces, ln_gains[0], qk_gains[0], half, 2, tuple(kept)
        )
        if half == 1:
            part = after(part, swapped[0][1])
        swapped.append((part, swap(part)))
    first_weights = pieces[0]
    if aligned:
        first_weights = assemble(none, [after(pieces[0], part)] + pieces[1:])
    for half in range(2):
        own = first_in[half * (number // 2) * pad : (half + 1) * (number // 2) * pad].astype(F32)
        part, arrived = swapped[half]
        middles.append((own + part.astype(F32) + after(arrived, first_weights).astype(F32)).astype(BF))
    middle = jnp.concatenate(middles)
    weights = [[first_weights], [second_weights]]

    grad = padded(cotangent)
    halves, last_parts, parts, theirs, sums_1 = [], [], [], [], 0
    for half in range(2):
        last_half, part, sums, normed, mixed, hidden, d_up, d_qkv = whole_block(
            tokens, units, place, middles[half], grad, weights[1][0], ln_gains[1], qk_gains[1], half, 2
        )
        own = slice(half * (number // 2) * pad, (half + 1) * (number // 2) * pad)
        halves.append((hidden, grad[own], normed, d_up, mixed, d_qkv))
        last_parts.append(last_half)
        parts.append(part)
        theirs.append(swap(part))
        sums_1 = sums_1 + sums
    halves[1] = (after(halves[1][0], theirs[0]),) + halves[1][1:]
    quarter = count // 4 * rows
    far = range(1, count // 4)

    def far_stage(total):
        return [total[:rows]] + [relative(total[step * rows : (step + 1) * rows], 4 * step) for step in far]

    spreads = weight_grads(place, units, halves, count if aligned else 0)
    if not aligned:
        spreads = [value for terms in spreads for value in spread_rows(terms, count, place)]
    spreads = beside(spreads, theirs[1])
    feed_second, attention_second = (
        add_low(mine, relative(sent, 1)) for mine, sent in (spreads[:2], spreads[2:])
    )
    feed_sent, attention_sent = feed_second[quarter:], attention_second[quarter:]
    feed_arrived = relative(feed_sent, 2)
    middle_grad = norm_backward(
        after(grad, feed_sent, attention_sent), middle, jnp.concatenate(parts), jnp.concatenate(theirs), ln_gains[1]
    )
    last_part = jnp.concatenate(last_parts)

    if aligned:
        feed_part, mine, sent = feed_back(place, units, count, middle_grad, weights[0][0], kept[0], *kept[6:])
    else:
        terms, feed_part = feed_backward(none, units, middle_grad, kept[0], weights[0], *kept[6:])
        mine, sent = spread_rows(terms, count, place)
    feed_second = add_low(feed_second[:quarter], beside((feed_arrived,), sent)[0])
    feed_second_terms = far_stage(feed_second)
    total = add_low(mine, relative(after(sent, feed_second), 1))
    sent = total[quarter:]
    arrived = relative(sent, 2)
    attention_in = after(middle_grad, sent, *feed_second_terms[:1])
    ln_inverse = 1.0 / jnp.concatenate(ln_gains, axis=0)
    if aligned:
        part, mine, sent = attention_back(
            tokens, place, count, attention_in, weights[0][0], qk_gains[0], ln_inverse, sums_1, *kept[:6], feed_part
        )
    else:
        terms, part, sums_0 = attention_backward(
            tokens, none, attention_in, weights[0], qk_gains[0], *kept[:6], feed_part
        )
        mine, sent = spread_rows(terms, count, place)
        gain_rows = jnp.zeros((16, SPLIT), F32)
        for block, sums in enumerate((sums_0, sums_1)):
            gain_rows = gain_rows.at[3 * block, :D].set(sums[0] * ln_inverse[block])
            for kind in range(2):
                value = sums[1:2, kind * HALF : (kind + 1) * HALF]
                gain_rows = lax.dynamic_update_slice(gain_rows, value, (3 * block + 1 + kind, section * HALF))
        mine, sent = (jnp.concatenate([value, gain_rows.astype(BF)], axis=0) for value in (mine, sent))
    far_total = add_low(total[:quarter], beside((arrived,), sent)[0])
    feed_terms = far_stage(far_total)
    feed_second_sum = add_all(beside(feed_second_terms, sent)).astype(BF)
    second_arrived = relative(after(attention_sent, far_total), 2)
    theirs = give(part, 1)
    last_theirs = give(after(last_part, part), 0)
    attention_total = add_low(mine, relative(after(sent, far_total, feed_second_sum), 1))
    attention_second = add_low(attention_second[:quarter], beside((second_arrived,), attention_total)[0])
    attention_second_terms = far_stage(attention_second)
    feed_sum = add_all(beside(feed_terms, attention_second)).astype(BF)
    attention_arrived = relative(after(attention_total[quarter:], attention_second, feed_sum, theirs, last_theirs), 2)
    feed_theirs = give(feed_sum, 1)
    feed_second_theirs = give(feed_second_sum, 0)
    total = attention_total
    attention_second_sum = add_all(beside(attention_second_terms, feed_sum)).astype(BF)
    attention_second_theirs = give(attention_second_sum, 0)
    arrived = after(attention_arrived, attention_second_sum)
    far_total = add_low(total[:quarter], arrived[:quarter])
    gain_total = add_low(total[2 * quarter :], arrived[quarter:])
    attention_terms = [jnp.concatenate([far_total[:rows], gain_total], axis=0)]
    for step in far:
        message = jnp.concatenate([far_total[step * rows : (step + 1) * rows], gain_total], axis=0)
        attention_terms.append(relative(message, 4 * step))
    attention_sum = add_all([after(attention_terms[0], attention_second_theirs, feed_theirs)] + attention_terms[1:]).astype(BF)
    attention_theirs = swap(attention_sum)
    second_sum = jnp.concatenate([attention_second_sum, feed_second_sum], axis=1)
    second_theirs = jnp.concatenate([attention_second_theirs, feed_second_theirs], axis=1)

    first_grad = norm_backward(middle_grad, first_in, after(part, attention_sum), theirs, ln_gains[0])
    input_grads = trimmed(jnp.where(first, first_grad, middle_grad))
    last_theirs = after(last_theirs, attention_sum)
    last = middle.astype(F32) + last_part.astype(F32) + last_theirs.astype(F32)
    outputs = trimmed(jnp.where(first, middle, last.astype(BF)))

    if aligned:
        grad_up, grad_down = finish(
            partial(finish_feed_kernel, count),
            "finish_feed",
            place,
            (feed_sum, feed_theirs, feed_second_sum, feed_second_theirs),
            ((rows, 2 * units), (4 * rows, D)),
        )
        grad_qkv, grad_proj, grad_ln, grad_q, grad_k = finish(
            finish_attention_kernel,
            "finish_attention",
            place,
            (attention_sum, attention_theirs, attention_second_sum, attention_second_theirs),
            ((rows, 3 * D), (rows, D), (1, D), (1, D), (1, D)),
        )
        return (
            outputs[None],
            input_grads[None],
            grad_qkv[None],
            grad_up[None],
            grad_proj[None],
            grad_down[None],
            grad_ln,
            grad_q,
            grad_k,
        )

    def halves_of(own, theirs):
        own, theirs = own.astype(F32), theirs.astype(F32)
        return jnp.where(first, own, theirs), jnp.where(first, theirs, own)

    own = jnp.where(first, feed_sum, second_sum[:, SPLIT:])
    other = jnp.where(first, feed_theirs, second_theirs[:, SPLIT:])
    ups, downs = [], []
    for source in halves_of(own, other):
        for part in range(2):
            at = part * D
            ups.append(source[:, at : at + D].reshape(rows, count, 1, group))
            downs.append(source[:, units + at : units + at + D])
    grad_up = jnp.concatenate(ups, axis=2).reshape(rows, 2 * units)
    grad_down = jnp.concatenate(downs, axis=0)

    own = jnp.where(first, attention_sum[:rows], second_sum[:, :SPLIT])
    other = jnp.where(first, attention_theirs[:rows], second_theirs[:, :SPLIT])
    low_half, high_half = halves_of(own, other)
    grad_proj = low_half[:, :D] + high_half[:, :D]
    pieces = []
    for pair in range(3):
        at = slice(D + pair * HALF, D + (pair + 1) * HALF)
        pieces += [low_half[:, at], high_half[:, at]]
    grad_qkv = jnp.concatenate(pieces, axis=1)
    totals = attention_sum[rows : rows + 6, :D].astype(F32) + attention_theirs[rows : rows + 6, :D].astype(F32)
    totals = jnp.where(first, totals[:3], totals[3:])
    return (
        outputs[None],
        input_grads[None],
        grad_qkv[None],
        grad_up[None],
        grad_proj[None],
        grad_down[None],
        totals[0:1],
        totals[1:2],
        totals[2:3],
    )


def solution(mesh):
    placed = (
        P("dp", None, None),
        P("dp", None, None),
        P("section", "dp", None),
        P("section", "dp", None),
        P("section", "dp", None),
        P("section", "dp", None),
        P("section", None),
        P("section", None),
        P("section", None),
    )
    return jax.shard_map(
        on_device,
        mesh=mesh,
        in_specs=placed,
        out_specs=(
            P("section", "dp", None, None),
            P("section", "dp", None, None),
            P("section", "dp", None),
            P("section", "dp", None),
            P("section", "dp", None),
            P("section", "dp", None),
            P("section", None),
            P("section", None),
            P("section", None),
        ),
        check_vma=False,
    )
```
